256 devices in a mesh: wide: 64 (over z, x, core), slab: 4 (over y).
Axes of the slice: x: 4, y: 4, z: 8, core: 2. Of those that a mesh axis runs over, the one named last changes fastest.
Arguments:
- fields: float32 [4, 512, 512, 512], P(None, 'slab', 'wide'), may hold values from -60 to 60
- start_basis: float32 [512, 128], replicated, may hold values from -6 to 6
Outputs:
- core_tensor: float32 [4, 512, 512, 128], P(None, None, ('wide', 'slab'))
The draws below stay inside these ranges and needn't reach their ends.
All inputs are finite; a program needn't handle non-finite values.
Results may differ from the reference program's by a relative error of at most 0.0003.
Values sent between devices are 32-bit elements; how exact they have to be, the bound alone decides.
A program may use at most 64 MiB of HBM per device.

```python
import jax
import jax.numpy as jnp
from jax import lax

N1 = 512
RANK = 128
NV = 4
SWEEPS = 4
N2 = 512
N3 = 512


def draw_fields(key, part):
    keys = jax.random.split(key, 4)
    scales = jnp.exp(jax.random.uniform(keys[0], (N1,), jnp.float32, 0.0, 1.7918))
    noise = jnp.clip(jax.random.normal(keys[1], (NV, N2, N3, N1), jnp.float32), -5.0, 5.0)
    loads = jnp.clip(0.3 * jax.random.normal(keys[2], (4, N1), jnp.float32), -1.5, 1.5)
    factors = jnp.clip(jax.random.normal(keys[3], (4, NV, N2, N3), jnp.float32), -4.0, 4.0)
    total = scales * noise
    total = total + factors[0][..., None] * loads[0]
    total = total + factors[1][..., None] * loads[1]
    total = total + factors[2][..., None] * loads[2]
    total = total + factors[3][..., None] * loads[3]
    return total.astype(jnp.float32)


def centred(own_key, extent, deviation, limit, held_as=jnp.bfloat16):
    return jnp.clip(deviation * jax.random.normal(own_key, extent, jnp.float32), -limit, limit).astype(held_as)


def setup_inputs(seed: int = 0) -> dict:
    key_list = jax.random.split(jax.random.key(seed), 3)
    return {
        "fields": draw_fields(jax.random.fold_in(key_list[2], 71), 0),
        "start_basis": centred(key_list[1], (N1, RANK), 1.0, 6.0, jnp.float32),
    }


def gram_of(unfolded, count):
    product = lax.dot_general(unfolded.astype(jnp.float32), unfolded.astype(jnp.float32), (((0,), (0,)), ((), ())), precision=lax.Precision.HIGHEST, preferred_element_type=jnp.float32)
    return product / count

def orthonormal(block):
    square = jnp.dot(block.T.astype(jnp.float32), block.astype(jnp.float32), precision=lax.Precision.HIGHEST, preferred_element_type=jnp.float32)
    triangle = jnp.linalg.cholesky(square)
    return lax.linalg.triangular_solve(triangle, block, left_side=False, lower=True, transpose_a=True)

def reference(fields, start_basis):
    unfolded = fields.reshape(-1, N1)
    gram = gram_of(unfolded, float(NV * N2 * N3))
    basis = start_basis
    for sweep in range(SWEEPS):
        block = jnp.dot(gram.astype(jnp.float32), basis.astype(jnp.float32), precision=lax.Precision.HIGHEST, preferred_element_type=jnp.float32)
        basis = orthonormal(block)
    projected = jnp.dot(unfolded.astype(jnp.float32), basis.astype(jnp.float32), precision=lax.Precision.HIGHEST, preferred_element_type=jnp.float32)
    return projected.reshape(NV, N2, N3, RANK)
```

```python
import jax
import jax.numpy as jnp
from jax import lax
from jax.experimental import pallas as pl
from jax.experimental.pallas import tpu as pltpu
from jax.sharding import PartitionSpec as P

SWEEPS = 4
MESH = pl.DeviceIdType.MESH
CORES, XS, ZS, YS = 2, 4, 8, 4
PLANE = XS * YS
N1 = 512
TILE = 128
PAIRS = [(i, j) for i in range(N1 // TILE) for j in range(i, N1 // TILE)]
HALF = len(PAIRS) // CORES
SHARE = HALF * TILE // PLANE
CHUNK = 512


def gram_kernel(x_hbm, g_ref, xbuf, s_ref, mine, theirs, inbox, total, parts, zparts, load_sem, core_sem, rs_send, rs_recv, z_send, z_recv,
                ag_send, ag_recv):
    wide = lax.axis_index("wide")
    y = lax.axis_index("slab")
    core = wide % CORES
    x = (wide // CORES) % XS
    z = wide // (CORES * XS)
    me = x * YS + y
    sibling = (wide + 1 - 2 * core, y)

    def plane_device(p):
        return ((z * XS + p // YS) * CORES + core, p % YS)

    def z_device(q):
        return ((q * XS + x) * CORES + core, y)

    barrier = pltpu.get_barrier_semaphore()
    pl.semaphore_signal(barrier, inc=1, device_id=sibling, device_id_type=MESH)
    for d in range(1, PLANE):
        pl.semaphore_signal(barrier, inc=1, device_id=plane_device((me + d) % PLANE), device_id_type=MESH)
    for d in range(1, ZS):
        pl.semaphore_signal(barrier, inc=1, device_id=z_device((z + d) % ZS), device_id_type=MESH)

    rows = x_hbm.shape[0]
    steps = rows // CHUNK

    def load(c):
        return pltpu.make_async_copy(x_hbm.at[pl.ds(c * CHUNK, CHUNK)], xbuf.at[pl.ds(c * CHUNK, CHUNK)], load_sem.at[c])

    for c in range(steps):
        load(c).start()
    s_ref[...] = jnp.zeros_like(s_ref)

    @pl.loop(0, steps)
    def _(c):
        load(c).wait()
        value = xbuf[pl.ds(pl.multiple_of(c * CHUNK, CHUNK), CHUNK), :]
        high = value.astype(jnp.bfloat16)
        low = (value - high.astype(jnp.float32)).astype(jnp.bfloat16)
        dims = (((0,), (0,)), ((), ()))
        s_ref[...] += 0.5 * lax.dot_general(high, high, dims, preferred_element_type=jnp.float32) + lax.dot_general(
            high, low, dims, preferred_element_type=jnp.float32)

    scale = 1.0 / (rows * PLANE * ZS * CORES)
    pl.semaphore_wait(barrier, PLANE + ZS - 1)

    def block(n):
        i, j = PAIRS[n]
        a = s_ref[i * TILE:(i + 1) * TILE, j * TILE:(j + 1) * TILE]
        b = s_ref[j * TILE:(j + 1) * TILE, i * TILE:(i + 1) * TILE]
        return (a + b.T) * scale

    for c in range(CORES):
        @pl.when(core == c)
        def _():
            for n in range(HALF):
                theirs[n * TILE:(n + 1) * TILE, :] = block((1 - c) * HALF + n)
                mine[n * TILE:(n + 1) * TILE, :] = block(c * HALF + n)

    swap = pltpu.make_async_remote_copy(theirs, inbox, core_sem.at[0], core_sem.at[1], device_id=sibling, device_id_type=MESH)
    swap.start()
    swap.wait()
    mine[...] += inbox[...]

    def scatter(p, source):
        return pltpu.make_async_remote_copy(
            mine.at[pl.ds(p * SHARE, SHARE)], parts.at[source], rs_send.at[p], rs_recv.at[source],
            device_id=plane_device(p), device_id_type=MESH)

    @pl.loop(1, PLANE)
    def _(d):
        scatter((me + d) % PLANE, me).start()

    own = zparts.at[z]
    own[...] = mine[pl.ds(pl.multiple_of(me * SHARE, 8), SHARE), :]

    @pl.loop(1, PLANE)
    def _(d):
        source = (me + PLANE - d) % PLANE
        scatter((me + d) % PLANE, source).wait_recv()
        own[...] += parts[source]

    def along_z(q, source):
        return pltpu.make_async_remote_copy(
            zparts.at[z], zparts.at[source], z_send.at[q], z_recv.at[source], device_id=z_device(q), device_id_type=MESH)

    for d in range(1, ZS):
        pltpu.make_async_remote_copy(
            zparts.at[z], zparts.at[z], z_send.at[(z + d) % ZS], z_recv.at[z], device_id=z_device((z + d) % ZS),
            device_id_type=MESH).start()
    for d in range(1, ZS):
        q = (z + d) % ZS
        pltpu.make_async_remote_copy(
            zparts.at[q], zparts.at[q], z_send.at[q], z_recv.at[q], device_id=z_device(q), device_id_type=MESH).wait_recv()
    value = zparts[0]
    for q in range(1, ZS):
        value = value + zparts[q]
    done = total.at[core]
    done[pl.ds(pl.multiple_of(me * SHARE, 8), SHARE), :] = value

    def gather(p, source):
        rows_ = pl.ds(source * SHARE, SHARE)
        return pltpu.make_async_remote_copy(
            done.at[rows_], done.at[rows_], ag_send.at[p], ag_recv.at[source], device_id=plane_device(p), device_id_type=MESH)

    @pl.loop(1, PLANE)
    def _(d):
        gather((me + d) % PLANE, me).start()

    @pl.loop(1, PLANE)
    def _(d):
        source = (me + PLANE - d) % PLANE
        gather((me + d) % PLANE, source).wait_recv()

    back = pltpu.make_async_remote_copy(done, done, core_sem.at[2], core_sem.at[3], device_id=sibling, device_id_type=MESH)
    back.start()
    back.wait()

    for n, (i, j) in enumerate(PAIRS):
        m = n % HALF
        value = total[n // HALF, m * TILE:(m + 1) * TILE, :]
        g_ref[i * TILE:(i + 1) * TILE, j * TILE:(j + 1) * TILE] = value
        if i != j:
            g_ref[j * TILE:(j + 1) * TILE, i * TILE:(i + 1) * TILE] = value.T

    @pl.loop(1, PLANE)
    def _(d):
        p = (me + d) % PLANE
        scatter(p, me).wait_send()
        gather(p, me).wait_send()

    for d in range(1, ZS):
        q = (z + d) % ZS
        pltpu.make_async_remote_copy(
            zparts.at[z], zparts.at[z], z_send.at[q], z_recv.at[z], device_id=z_device(q), device_id_type=MESH).wait_send()


def reduced_gram(unfolded):
    rows, n1 = unfolded.shape
    steps = rows // CHUNK
    return pl.pallas_call(
        gram_kernel,
        out_shape=jax.ShapeDtypeStruct((n1, n1), jnp.float32),
        in_specs=[pl.BlockSpec(memory_space=pl.ANY)],
        out_specs=pl.BlockSpec(memory_space=pltpu.VMEM),
        scratch_shapes=[
            pltpu.VMEM((rows, n1), jnp.float32),
            pltpu.VMEM((n1, n1), jnp.float32),
            pltpu.VMEM((HALF * TILE, TILE), jnp.float32),
            pltpu.VMEM((HALF * TILE, TILE), jnp.float32),
            pltpu.VMEM((HALF * TILE, TILE), jnp.float32),
            pltpu.VMEM((CORES, HALF * TILE, TILE), jnp.float32),
            pltpu.VMEM((PLANE, SHARE, TILE), jnp.float32),
            pltpu.VMEM((ZS, SHARE, TILE), jnp.float32),
            pltpu.SemaphoreType.DMA((steps,)),
            pltpu.SemaphoreType.DMA((4,)),
            pltpu.SemaphoreType.DMA((PLANE,)),
            pltpu.SemaphoreType.DMA((PLANE,)),
            pltpu.SemaphoreType.DMA((ZS,)),
            pltpu.SemaphoreType.DMA((ZS,)),
            pltpu.SemaphoreType.DMA((PLANE,)),
            pltpu.SemaphoreType.DMA((PLANE,)),
        ],
        compiler_params=pltpu.CompilerParams(collective_id=0, has_side_effects=True, vmem_limit_bytes=48 << 20),
    )(unfolded)


def orthonormal(block):
    square = jnp.dot(
        block.T, block, precision=lax.Precision.HIGHEST, preferred_element_type=jnp.float32
    )
    triangle = jnp.linalg.cholesky(square)
    return lax.linalg.triangular_solve(
        triangle, block, left_side=False, lower=True, transpose_a=True
    )


def per_device(fields, start_basis):
    unfolded = fields.reshape(-1, fields.shape[-1])
    gram = reduced_gram(unfolded)
    basis = start_basis
    for sweep in range(SWEEPS):
        block = jnp.dot(
            gram, basis, precision=lax.Precision.HIGHEST, preferred_element_type=jnp.float32
        )
        basis = orthonormal(block)
    projected = jnp.dot(
        unfolded, basis, precision=lax.Precision.HIGHEST, preferred_element_type=jnp.float32
    )
    projected = projected.reshape(fields.shape[0], fields.shape[1], fields.shape[2], basis.shape[1])
    return lax.all_to_all(projected, "slab", split_axis=2, concat_axis=1, tiled=True)


def solution(mesh):
    in_specs = (P(None, "slab", "wide", None), P())
    out_specs = P(None, None, ("wide", "slab"), None)
    return jax.shard_map(
        per_device, mesh=mesh, in_specs=in_specs, out_specs=out_specs, check_vma=False
    )
```

```python
import functools

import jax
import jax.numpy as jnp
from jax import lax
from jax.experimental import pallas as pl
from jax.experimental.pallas import tpu as pltpu
from jax.sharding import PartitionSpec as P

SWEEPS = 4
MESH = pl.DeviceIdType.MESH
CORES, XS, ZS, YS = 2, 4, 8, 4
PLANE = XS * YS
N1 = 512
TILE = 128
PAIRS = [(i, j) for i in range(N1 // TILE) for j in range(i, N1 // TILE)]
HALF = len(PAIRS) // CORES
SHARE = HALF * TILE // PLANE
CHUNK = 512
SUB = 8
RANK = 128
HIGHEST = lax.Precision.HIGHEST
NT = (((1,), (1,)), ((), ()))
TN = (((0,), (0,)), ((), ()))
NN = (((1,), (0,)), ((), ()))


def inverse_factor(square, n):
    blocks = n // SUB
    lane = lax.broadcasted_iota(jnp.int32, (SUB, n), 1)
    sub = lax.broadcasted_iota(jnp.int32, (SUB, n), 0)
    a = [square[SUB * i:SUB * (i + 1), :] for i in range(blocks)]
    j = [(lane == sub + SUB * i).astype(jnp.float32) for i in range(blocks)]
    rows = []

    def along_lanes(v, c):
        return jnp.broadcast_to(v[:, c:c + 1], (SUB, n))

    def along_sublanes(v, p):
        return jnp.broadcast_to(v[p:p + 1, :], (SUB, n))

    for k in range(blocks):
        cols = [along_lanes(a[k], SUB * k + p) for p in range(SUB)]
        e = {(i, p): along_sublanes(cols[p], i) for p in range(SUB) for i in range(p, SUB)}
        r, l = [], {}
        for p in range(SUB):
            r.append(lax.rsqrt(e[p, p]))
            for i in range(p + 1, SUB):
                l[i, p] = e[i, p] * r[p]
            for q in range(p + 1, SUB):
                for i in range(q, SUB):
                    e[i, q] = e[i, q] - l[i, p] * l[q, p]

        def forward(values):
            out = []
            for p in range(SUB):
                v = values[p]
                for q in range(p):
                    v = v - l[p, q] * out[q]
                out.append(v * r[p])
            return out

        upper = forward([along_sublanes(a[k], p) for p in range(SUB)])
        inverse = forward([along_sublanes(j[k], p) for p in range(SUB)])
        rows.extend(v[:1] for v in inverse)
        for i in range(k + 1, blocks):
            lower = forward([along_lanes(a[i], SUB * k + p) for p in range(SUB)])
            for p in range(SUB):
                a[i] = a[i] - lower[p] * upper[p]
                j[i] = j[i] - lower[p] * inverse[p]
    return rows


def tucker_kernel(nv, x_hbm, start_ref, out_ref, xbuf, high_ref, low_ref, g_ref, basis_ref, product_ref, outbox, s_ref, mine, theirs, inbox, total, parts, zparts, load_sem, core_sem, rs_send, rs_recv, z_send, z_recv,
                ag_send, ag_recv, out_send, out_recv):
    wide = lax.axis_index("wide")
    y = lax.axis_index("slab")
    core = wide % CORES
    x = (wide // CORES) % XS
    z = wide // (CORES * XS)
    me = x * YS + y
    sibling = (wide + 1 - 2 * core, y)

    def plane_device(p):
        return ((z * XS + p // YS) * CORES + core, p % YS)

    def z_device(q):
        return ((q * XS + x) * CORES + core, y)

    barrier = pltpu.get_barrier_semaphore()
    pl.semaphore_signal(barrier, inc=1, device_id=sibling, device_id_type=MESH)
    for d in range(1, PLANE):
        pl.semaphore_signal(barrier, inc=1, device_id=plane_device((me + d) % PLANE), device_id_type=MESH)
    for d in range(1, ZS):
        pl.semaphore_signal(barrier, inc=1, device_id=z_device((z + d) % ZS), device_id_type=MESH)

    rows = x_hbm.shape[0]
    steps = rows // CHUNK

    def load(c):
        return pltpu.make_async_copy(x_hbm.at[pl.ds(c * CHUNK, CHUNK)], xbuf.at[pl.ds(c * CHUNK, CHUNK)], load_sem.at[c])

    for c in range(steps):
        load(c).start()
    s_ref[...] = jnp.zeros_like(s_ref)

    @pl.loop(0, steps)
    def _(c):
        load(c).wait()
        rows_ = pl.ds(pl.multiple_of(c * CHUNK, CHUNK), CHUNK)
        value = xbuf[rows_, :]
        high = value.astype(jnp.bfloat16)
        low = (value - high.astype(jnp.float32)).astype(jnp.bfloat16)
        high_ref[rows_, :] = high
        low_ref[rows_, :] = low
        s_ref[...] += 0.5 * lax.dot_general(high, high, TN, preferred_element_type=jnp.float32) + lax.dot_general(
            high, low, TN, preferred_element_type=jnp.float32)

    basis_ref[...] = start_ref[...].T
    scale = 1.0 / (rows * PLANE * ZS * CORES)
    pl.semaphore_wait(barrier, PLANE + ZS - 1)

    def block(n):
        i, j = PAIRS[n]
        a = s_ref[i * TILE:(i + 1) * TILE, j * TILE:(j + 1) * TILE]
        b = s_ref[j * TILE:(j + 1) * TILE, i * TILE:(i + 1) * TILE]
        return (a + b.T) * scale

    for c in range(CORES):
        @pl.when(core == c)
        def _():
            for n in range(HALF):
                theirs[n * TILE:(n + 1) * TILE, :] = block((1 - c) * HALF + n)
                mine[n * TILE:(n + 1) * TILE, :] = block(c * HALF + n)

    swap = pltpu.make_async_remote_copy(theirs, inbox, core_sem.at[0], core_sem.at[1], device_id=sibling, device_id_type=MESH)
    swap.start()
    swap.wait()
    mine[...] += inbox[...]

    def scatter(p, source):
        return pltpu.make_async_remote_copy(
            mine.at[pl.ds(p * SHARE, SHARE)], parts.at[source], rs_send.at[p], rs_recv.at[source],
            device_id=plane_device(p), device_id_type=MESH)

    @pl.loop(1, PLANE)
    def _(d):
        scatter((me + d) % PLANE, me).start()

    own = zparts.at[z]
    own[...] = mine[pl.ds(pl.multiple_of(me * SHARE, 8), SHARE), :]

    @pl.loop(1, PLANE)
    def _(d):
        source = (me + PLANE - d) % PLANE
        scatter((me + d) % PLANE, source).wait_recv()
        own[...] += parts[source]

    def along_z(q, source):
        return pltpu.make_async_remote_copy(
            zparts.at[z], zparts.at[source], z_send.at[q], z_recv.at[source], device_id=z_device(q), device_id_type=MESH)

    for d in range(1, ZS):
        pltpu.make_async_remote_copy(
            zparts.at[z], zparts.at[z], z_send.at[(z + d) % ZS], z_recv.at[z], device_id=z_device((z + d) % ZS),
            device_id_type=MESH).start()
    for d in range(1, ZS):
        q = (z + d) % ZS
        pltpu.make_async_remote_copy(
            zparts.at[q], zparts.at[q], z_send.at[q], z_recv.at[q], device_id=z_device(q), device_id_type=MESH).wait_recv()
    value = zparts[0]
    for q in range(1, ZS):
        value = value + zparts[q]
    done = total.at[core]
    done[pl.ds(pl.multiple_of(me * SHARE, 8), SHARE), :] = value

    def gather(p, source):
        rows_ = pl.ds(source * SHARE, SHARE)
        return pltpu.make_async_remote_copy(
            done.at[rows_], done.at[rows_], ag_send.at[p], ag_recv.at[source], device_id=plane_device(p), device_id_type=MESH)

    @pl.loop(1, PLANE)
    def _(d):
        gather((me + d) % PLANE, me).start()

    @pl.loop(1, PLANE)
    def _(d):
        source = (me + PLANE - d) % PLANE
        gather((me + d) % PLANE, source).wait_recv()

    back = pltpu.make_async_remote_copy(done, done, core_sem.at[2], core_sem.at[3], device_id=sibling, device_id_type=MESH)
    back.start()
    back.wait()

    for n, (i, j) in enumerate(PAIRS):
        m = n % HALF
        value = total[n // HALF, m * TILE:(m + 1) * TILE, :]
        g_ref[i * TILE:(i + 1) * TILE, j * TILE:(j + 1) * TILE] = value
        if i != j:
            g_ref[j * TILE:(j + 1) * TILE, i * TILE:(i + 1) * TILE] = value.T

    @pl.loop(0, SWEEPS)
    def _(sweep):
        block = lax.dot_general(basis_ref[...], g_ref[...], NN, precision=HIGHEST, preferred_element_type=jnp.float32)
        square = lax.dot_general(block, block, NT, precision=HIGHEST, preferred_element_type=jnp.float32)
        for n, row in enumerate(inverse_factor(square, RANK)):
            s_ref[n:n + 1, :RANK] = row
        basis_ref[...] = lax.dot_general(s_ref[:RANK, :RANK], block, NN, precision=HIGHEST, preferred_element_type=jnp.float32)

    basis = basis_ref[...]
    basis_high = basis.astype(jnp.bfloat16)
    basis_low = (basis - basis_high.astype(jnp.float32)).astype(jnp.bfloat16)
    both = jnp.concatenate([basis_high, basis_low], axis=0)
    pairs = CHUNK // YS
    halves = steps // nv

    def send(c, p, source):
        return pltpu.make_async_remote_copy(
            outbox.at[p, pl.ds(c * pairs, pairs)],
            out_ref.at[c // halves, pl.ds((source * halves + c % halves) * pairs, pairs)],
            out_send.at[c, p], out_recv.at[c, source], device_id=(wide, p), device_id_type=MESH)

    @pl.loop(0, steps)
    def _(c):
        rows_ = pl.ds(pl.multiple_of(c * CHUNK, CHUNK), CHUNK)
        wideproduct = lax.dot_general(high_ref[rows_, :], both, NT, preferred_element_type=jnp.float32)
        product_ref[...] = wideproduct[:, :RANK] + (wideproduct[:, RANK:] + lax.dot_general(
            low_ref[rows_, :], basis_high, NT, preferred_element_type=jnp.float32))
        width = 2 * YS
        count = CHUNK // width
        for p in range(YS):
            for i in range(2):
                outbox[p, pl.ds(c * pairs + i, count, stride=2), :] = product_ref[pl.ds(2 * p + i, count, stride=width), :]
        for d in (2, 1, 3):
            send(c, (y + d) % YS, y).start()
        out_ref[c // halves, pl.ds(pl.multiple_of((y * halves + c % halves) * pairs, pairs), pairs), :] = outbox[
            y, pl.ds(pl.multiple_of(c * pairs, pairs), pairs), :]

    @pl.loop(0, steps)
    def _(c):
        for d in (2, 1, 3):
            send(c, (y + d) % YS, (y + YS - d) % YS).wait_recv()

    @pl.loop(0, steps)
    def _(c):
        for d in (2, 1, 3):
            send(c, (y + d) % YS, y).wait_send()

    @pl.loop(1, PLANE)
    def _(d):
        p = (me + d) % PLANE
        scatter(p, me).wait_send()
        gather(p, me).wait_send()

    for d in range(1, ZS):
        q = (z + d) % ZS
        pltpu.make_async_remote_copy(
            zparts.at[z], zparts.at[z], z_send.at[q], z_recv.at[z], device_id=z_device(q), device_id_type=MESH).wait_send()


def per_device(fields, start_basis):
    nv, n2, n3, n1 = fields.shape
    unfolded = fields.reshape(-1, n1)
    rows = unfolded.shape[0]
    steps = rows // CHUNK
    out = pl.pallas_call(
        functools.partial(tucker_kernel, nv),
        out_shape=jax.ShapeDtypeStruct((nv, rows // nv, RANK), jnp.float32),
        in_specs=[pl.BlockSpec(memory_space=pl.ANY), pl.BlockSpec(memory_space=pltpu.VMEM)],
        out_specs=pl.BlockSpec(memory_space=pltpu.VMEM),
        scratch_shapes=[
            pltpu.VMEM((rows, n1), jnp.float32),
            pltpu.VMEM((rows, n1), jnp.bfloat16),
            pltpu.VMEM((rows, n1), jnp.bfloat16),
            pltpu.VMEM((n1, n1), jnp.float32),
            pltpu.VMEM((RANK, n1), jnp.float32),
            pltpu.VMEM((CHUNK, RANK), jnp.float32),
            pltpu.VMEM((YS, rows // YS, RANK), jnp.float32),
            pltpu.VMEM((n1, n1), jnp.float32),
            pltpu.VMEM((HALF * TILE, TILE), jnp.float32),
            pltpu.VMEM((HALF * TILE, TILE), jnp.float32),
            pltpu.VMEM((HALF * TILE, TILE), jnp.float32),
            pltpu.VMEM((CORES, HALF * TILE, TILE), jnp.float32),
            pltpu.VMEM((PLANE, SHARE, TILE), jnp.float32),
            pltpu.VMEM((ZS, SHARE, TILE), jnp.float32),
            pltpu.SemaphoreType.DMA((steps,)),
            pltpu.SemaphoreType.DMA((4,)),
            pltpu.SemaphoreType.DMA((PLANE,)),
            pltpu.SemaphoreType.DMA((PLANE,)),
            pltpu.SemaphoreType.DMA((ZS,)),
            pltpu.SemaphoreType.DMA((ZS,)),
            pltpu.SemaphoreType.DMA((PLANE,)),
            pltpu.SemaphoreType.DMA((PLANE,)),
            pltpu.SemaphoreType.DMA((steps, YS)),
            pltpu.SemaphoreType.DMA((steps, YS)),
        ],
        compiler_params=pltpu.CompilerParams(collective_id=0, has_side_effects=True, vmem_limit_bytes=56 << 20),
    )(unfolded, start_basis)
    return out.reshape(nv, n2 * YS, n3 // YS, RANK)


def solution(mesh):
    in_specs = (P(None, "slab", "wide", None), P())
    out_specs = P(None, None, ("wide", "slab"), None)
    return jax.shard_map(
        per_device, mesh=mesh, in_specs=in_specs, out_specs=out_specs, check_vma=False
    )
```

```python
import functools

import jax
import jax.numpy as jnp
from jax import lax
from jax.experimental import pallas as pl
from jax.experimental.pallas import tpu as pltpu
from jax.sharding import PartitionSpec as P

SWEEPS = 4
MESH = pl.DeviceIdType.MESH
CORES, XS, ZS, YS = 2, 4, 8, 4
PLANE = XS * YS
N1 = 512
TILE = 128
PAIRS = [(i, j) for i in range(N1 // TILE) for j in range(i, N1 // TILE)]
HALF = len(PAIRS) // CORES
OWN = TILE // PLANE
GROUPS = ((0, 3), (3, HALF))
CHUNK = 512
SUB = 8
RANK = 128
HIGHEST = lax.Precision.HIGHEST
NT = (((1,), (1,)), ((), ()))
TN = (((0,), (0,)), ((), ()))
NN = (((1,), (0,)), ((), ()))


def inverse_factor(square, n):
    blocks = n // SUB
    lane = lax.broadcasted_iota(jnp.int32, (SUB, n), 1)
    sub = lax.broadcasted_iota(jnp.int32, (SUB, n), 0)
    a = [square[SUB * i:SUB * (i + 1), :] for i in range(blocks)]
    j = [(lane == sub + SUB * i).astype(jnp.float32) for i in range(blocks)]
    rows = []

    def along_lanes(v, c):
        return jnp.broadcast_to(v[:, c:c + 1], (SUB, n))

    def along_sublanes(v, p):
        return jnp.broadcast_to(v[p:p + 1, :], (SUB, n))

    for k in range(blocks):
        cols = [along_lanes(a[k], SUB * k + p) for p in range(SUB)]
        e = {(i, p): along_sublanes(cols[p], i) for p in range(SUB) for i in range(p, SUB)}
        r, l = [], {}
        for p in range(SUB):
            r.append(lax.rsqrt(e[p, p]))
            for i in range(p + 1, SUB):
                l[i, p] = e[i, p] * r[p]
            for q in range(p + 1, SUB):
                for i in range(q, SUB):
                    e[i, q] = e[i, q] - l[i, p] * l[q, p]

        def forward(values):
            out = []
            for p in range(SUB):
                v = values[p]
                for q in range(p):
                    v = v - l[p, q] * out[q]
                out.append(v * r[p])
            return out

        upper = forward([along_sublanes(a[k], p) for p in range(SUB)])
        inverse = forward([along_sublanes(j[k], p) for p in range(SUB)])
        rows.extend(v[:1] for v in inverse)
        for i in range(k + 1, blocks):
            lower = forward([along_lanes(a[i], SUB * k + p) for p in range(SUB)])
            for p in range(SUB):
                a[i] = a[i] - lower[p] * upper[p]
                j[i] = j[i] - lower[p] * inverse[p]
    return rows


def tucker_kernel(nv, x_hbm, start_ref, y_ref, factor_ref, xbuf, g_ref, basis_ref, block_ref, last_ref, product_ref, outbox, s_ref, mine,
                  theirs, inbox, total, parts, zparts, load_sem, swap_sem, rs_send, rs_recv, z_send, z_recv, ag_send, ag_recv,
                  back_sem, out_send, out_recv, keep_sem):
    wide = lax.axis_index("wide")
    y = lax.axis_index("slab")
    core = wide % CORES
    x = (wide // CORES) % XS
    z = wide // (CORES * XS)
    me = x * YS + y
    sibling = (wide + 1 - 2 * core, y)
    groups = range(len(GROUPS))

    def plane_device(p):
        return ((z * XS + p // YS) * CORES + core, p % YS)

    def z_device(q):
        return ((q * XS + x) * CORES + core, y)

    barrier = pltpu.get_barrier_semaphore()
    pl.semaphore_signal(barrier, inc=1, device_id=sibling, device_id_type=MESH)

    @pl.loop(1, PLANE)
    def _(d):
        pl.semaphore_signal(barrier, inc=1, device_id=plane_device((me + d) % PLANE), device_id_type=MESH)

    @pl.loop(1, ZS)
    def _(d):
        pl.semaphore_signal(barrier, inc=1, device_id=z_device((z + d) % ZS), device_id_type=MESH)

    rows = x_hbm.shape[0]
    steps = rows // CHUNK

    def load(c):
        return pltpu.make_async_copy(x_hbm.at[pl.ds(c * CHUNK, CHUNK)], xbuf.at[pl.ds(c * CHUNK, CHUNK)], load_sem.at[c])

    for c in range(steps):
        load(c).start()
    s_ref[...] = jnp.zeros_like(s_ref)
    basis_ref[...] = start_ref[...].T

    @pl.loop(0, steps)
    def _(c):
        load(c).wait()
        value = xbuf[pl.ds(pl.multiple_of(c * CHUNK, CHUNK), CHUNK), :]
        high = value.astype(jnp.bfloat16)
        low = (value - high.astype(jnp.float32)).astype(jnp.bfloat16)
        s_ref[...] += 0.5 * lax.dot_general(high, high, TN, preferred_element_type=jnp.float32) + lax.dot_general(
            high, low, TN, preferred_element_type=jnp.float32)

    scale = 1.0 / (rows * PLANE * ZS * CORES)
    pl.semaphore_wait(barrier, PLANE + ZS - 1)

    def block(n):
        i, j = PAIRS[n]
        a = s_ref[i * TILE:(i + 1) * TILE, j * TILE:(j + 1) * TILE]
        b = s_ref[j * TILE:(j + 1) * TILE, i * TILE:(i + 1) * TILE]
        return (a + b.T) * scale

    def span(g):
        first, last = GROUPS[g]
        return pl.ds(first * TILE, (last - first) * TILE)

    def share(g):
        first, last = GROUPS[g]
        return pl.ds(first * OWN, (last - first) * OWN)

    def owned(g, p):
        first, last = GROUPS[g]
        return pl.ds(pl.multiple_of(first * TILE + p * ((last - first) * OWN), SUB), (last - first) * OWN)

    def swap(g):
        return pltpu.make_async_remote_copy(
            theirs.at[span(g)], inbox.at[span(g)], swap_sem.at[0, g], swap_sem.at[1, g], device_id=sibling, device_id_type=MESH)

    for g in groups:
        for c in range(CORES):
            @pl.when(core == c)
            def _():
                for n in range(*GROUPS[g]):
                    theirs[n * TILE:(n + 1) * TILE, :] = block((1 - c) * HALF + n)
        swap(g).start()
    for c in range(CORES):
        @pl.when(core == c)
        def _():
            for n in range(HALF):
                mine[n * TILE:(n + 1) * TILE, :] = block(c * HALF + n)

    def scatter(g, p, source):
        return pltpu.make_async_remote_copy(
            mine.at[owned(g, p)], parts.at[source, share(g)], rs_send.at[g, p], rs_recv.at[g, source],
            device_id=plane_device(p), device_id_type=MESH)

    def along_z(g, q, source):
        return pltpu.make_async_remote_copy(
            zparts.at[source, share(g)], zparts.at[source, share(g)], z_send.at[g, q], z_recv.at[g, source],
            device_id=z_device(q), device_id_type=MESH)

    done = total.at[core]

    def gather(g, p, source):
        return pltpu.make_async_remote_copy(
            done.at[owned(g, source)], done.at[owned(g, source)], ag_send.at[g, p], ag_recv.at[g, source],
            device_id=plane_device(p), device_id_type=MESH)

    def back(g, c):
        return pltpu.make_async_remote_copy(
            total.at[c, span(g)], total.at[c, span(g)], back_sem.at[0, g], back_sem.at[1, g], device_id=sibling, device_id_type=MESH)

    for g in groups:
        swap(g).wait_recv()
        mine[span(g), :] += inbox[span(g), :]

        @pl.loop(1, PLANE)
        def _(d):
            scatter(g, (me + d) % PLANE, me).start()

    for g in groups:
        zparts[z, share(g), :] = mine[owned(g, me), :]

        @pl.loop(1, PLANE)
        def _(d):
            source = (me + PLANE - d) % PLANE
            scatter(g, (me + d) % PLANE, source).wait_recv()
            zparts[z, share(g), :] += parts[source, share(g), :]

        @pl.loop(1, ZS)
        def _(d):
            along_z(g, (z + d) % ZS, z).start()

    for g in groups:
        @pl.loop(1, ZS)
        def _(d):
            along_z(g, (z + d) % ZS, (z + ZS - d) % ZS).wait_recv()

        value = zparts[0, share(g), :]
        for q in range(1, ZS):
            value = value + zparts[q, share(g), :]
        done[owned(g, me), :] = value

        @pl.loop(1, PLANE)
        def _(d):
            gather(g, (me + d) % PLANE, me).start()

    for g in groups:
        @pl.loop(1, PLANE)
        def _(d):
            gather(g, (me + d) % PLANE, (me + PLANE - d) % PLANE).wait_recv()

        back(g, core).start()

    for g in groups:
        back(g, 1 - core).wait_recv()
        for half in range(CORES):
            for m in range(*GROUPS[g]):
                i, j = PAIRS[half * HALF + m]
                value = total[half, m * TILE:(m + 1) * TILE, :]
                g_ref[i * TILE:(i + 1) * TILE, j * TILE:(j + 1) * TILE] = value
                if i != j:
                    g_ref[j * TILE:(j + 1) * TILE, i * TILE:(i + 1) * TILE] = value.T

    def times(a, b, dims):
        return lax.dot_general(a, b, dims, precision=HIGHEST, preferred_element_type=jnp.float32)

    def inverse_triangle(block_):
        for n, row in enumerate(inverse_factor(times(block_, block_, NT), RANK)):
            s_ref[n:n + 1, :RANK] = row
        return s_ref[:RANK, :RANK]

    @pl.loop(0, SWEEPS - 2)
    def _(sweep):
        block_ref[...] = times(basis_ref[...], g_ref[...], NN)
        basis_ref[...] = times(inverse_triangle(block_ref[...]), block_ref[...], NN)

    block_ref[...] = times(basis_ref[...], g_ref[...], NN)
    last_ref[...] = times(block_ref[...], g_ref[...], NN)
    pairs = CHUNK // YS
    halves = steps // nv

    def place(c, source):
        return y_ref.at[c // halves, pl.ds((source * halves + c % halves) * pairs, pairs)]

    def send(c, p, source):
        return pltpu.make_async_remote_copy(
            outbox.at[p, pl.ds(c * pairs, pairs)], place(c, source), out_send.at[c, p], out_recv.at[c, source],
            device_id=(wide, p), device_id_type=MESH)

    def keep(c):
        return pltpu.make_async_copy(outbox.at[y, pl.ds(c * pairs, pairs)], place(c, y), keep_sem.at[c])

    @pl.loop(0, steps)
    def _(c):
        product_ref[...] = times(xbuf[pl.ds(pl.multiple_of(c * CHUNK, CHUNK), CHUNK), :], last_ref[...], NT)
        width = 2 * YS
        count = CHUNK // width
        for p in range(YS):
            for i in range(2):
                outbox[p, pl.ds(c * pairs + i, count, stride=2), :] = product_ref[pl.ds(2 * p + i, count, stride=width), :]
        for d in (2, 1, 3):
            send(c, (y + d) % YS, y).start()
        keep(c).start()

    factor_ref[...] = jnp.zeros_like(factor_ref)

    @pl.loop(0, 2)
    def _(sweep):
        inverse = inverse_triangle(block_ref[...])

        @pl.when(sweep == 0)
        def _():
            factor_ref[...] = inverse
            block_ref[...] = times(inverse, last_ref[...], NN)

        @pl.when(sweep == 1)
        def _():
            factor_ref[...] = times(inverse, factor_ref[...], NN)

    for g in groups:
        swap(g).wait_send()
        back(g, core).wait_send()

        @pl.loop(1, PLANE)
        def _(d):
            p = (me + d) % PLANE
            scatter(g, p, me).wait_send()
            gather(g, p, me).wait_send()

        @pl.loop(1, ZS)
        def _(d):
            along_z(g, (z + d) % ZS, z).wait_send()

    @pl.loop(0, steps)
    def _(c):
        keep(c).wait()
        for d in (2, 1, 3):
            send(c, (y + d) % YS, y).wait_send()
            send(c, (y + d) % YS, (y + YS - d) % YS).wait_recv()


def finish_kernel(y_ref, factor_ref, out_hbm, out_ref, sem):
    nv = y_ref.shape[0]

    def store(v):
        return pltpu.make_async_copy(out_ref.at[v], out_hbm.at[v], sem.at[v])

    for v in range(nv):
        out_ref[v] = lax.dot_general(y_ref[v], factor_ref[...], NT, precision=HIGHEST, preferred_element_type=jnp.float32)
        store(v).start()
    for v in range(nv):
        store(v).wait()


def per_device(fields, start_basis):
    nv, n2, n3, n1 = fields.shape
    unfolded = fields.reshape(-1, n1)
    rows = unfolded.shape[0]
    steps = rows // CHUNK
    stages = len(GROUPS)
    y, factor = pl.pallas_call(
        functools.partial(tucker_kernel, nv),
        out_shape=[jax.ShapeDtypeStruct((nv, rows // nv, RANK), jnp.float32), jax.ShapeDtypeStruct((RANK, RANK), jnp.float32)],
        in_specs=[pl.BlockSpec(memory_space=pl.ANY), pl.BlockSpec(memory_space=pltpu.VMEM)],
        out_specs=[pl.BlockSpec(memory_space=pl.ANY), pl.BlockSpec(memory_space=pltpu.VMEM)],
        scratch_shapes=[
            pltpu.VMEM((rows, n1), jnp.float32),
            pltpu.VMEM((n1, n1), jnp.float32),
            pltpu.VMEM((RANK, n1), jnp.float32),
            pltpu.VMEM((RANK, n1), jnp.float32),
            pltpu.VMEM((RANK, n1), jnp.float32),
            pltpu.VMEM((CHUNK, RANK), jnp.float32),
            pltpu.VMEM((YS, rows // YS, RANK), jnp.float32),
            pltpu.VMEM((n1, n1), jnp.float32),
            pltpu.VMEM((HALF * TILE, TILE), jnp.float32),
            pltpu.VMEM((HALF * TILE, TILE), jnp.float32),
            pltpu.VMEM((HALF * TILE, TILE), jnp.float32),
            pltpu.VMEM((CORES, HALF * TILE, TILE), jnp.float32),
            pltpu.VMEM((PLANE, HALF * OWN, TILE), jnp.float32),
            pltpu.VMEM((ZS, HALF * OWN, TILE), jnp.float32),
            pltpu.SemaphoreType.DMA((steps,)),
            pltpu.SemaphoreType.DMA((2, stages)),
            pltpu.SemaphoreType.DMA((stages, PLANE)),
            pltpu.SemaphoreType.DMA((stages, PLANE)),
            pltpu.SemaphoreType.DMA((stages, ZS)),
            pltpu.SemaphoreType.DMA((stages, ZS)),
            pltpu.SemaphoreType.DMA((stages, PLANE)),
            pltpu.SemaphoreType.DMA((stages, PLANE)),
            pltpu.SemaphoreType.DMA((2, stages)),
            pltpu.SemaphoreType.DMA((steps, YS)),
            pltpu.SemaphoreType.DMA((steps, YS)),
            pltpu.SemaphoreType.DMA((steps,)),
        ],
        compiler_params=pltpu.CompilerParams(collective_id=0, has_side_effects=True, vmem_limit_bytes=48 << 20),
    )(unfolded, start_basis)
    out = pl.pallas_call(
        finish_kernel,
        out_shape=jax.ShapeDtypeStruct(y.shape, jnp.float32),
        in_specs=[pl.BlockSpec(memory_space=pltpu.VMEM)] * 2,
        out_specs=pl.BlockSpec(memory_space=pl.ANY),
        scratch_shapes=[pltpu.VMEM(y.shape, jnp.float32), pltpu.SemaphoreType.DMA((nv,))],
    )(y, factor)
    return out.reshape(nv, n2 * YS, n3 // YS, RANK)


def solution(mesh):
    in_specs = (P(None, "slab", "wide", None), P())
    out_specs = P(None, None, ("wide", "slab"), None)
    return jax.shard_map(
        per_device, mesh=mesh, in_specs=in_specs, out_specs=out_specs, check_vma=False
    )
```

```python
import functools

import jax
import jax.numpy as jnp
from jax import lax
from jax.experimental import pallas as pl
from jax.experimental.pallas import tpu as pltpu
from jax.sharding import PartitionSpec as P

SWEEPS = 4
MESH = pl.DeviceIdType.MESH
CORES, XS, ZS, YS = 2, 4, 8, 4
PLANE = XS * YS
N1 = 512
TILE = 128
PAIRS = [(i, j) for i in range(N1 // TILE) for j in range(i, N1 // TILE)]
HALF = len(PAIRS) // CORES
OWN = TILE // PLANE
GROUPS = ((0, 3), (3, HALF))
CHUNK = 512
SUB = 8
RAW = 2
RANK = 128
HIGHEST = lax.Precision.HIGHEST
NT = (((1,), (1,)), ((), ()))
TN = (((0,), (0,)), ((), ()))
NN = (((1,), (0,)), ((), ()))


def inverse_factor(square, n):
    blocks = n // SUB
    lane = lax.broadcasted_iota(jnp.int32, (SUB, n), 1)
    sub = lax.broadcasted_iota(jnp.int32, (SUB, n), 0)
    a = [square[SUB * i:SUB * (i + 1), :] for i in range(blocks)]
    j = [(lane == sub + SUB * i).astype(jnp.float32) for i in range(blocks)]
    rows = []

    def along_lanes(v, c):
        return jnp.broadcast_to(v[:, c:c + 1], (SUB, n))

    def along_sublanes(v, p):
        return jnp.broadcast_to(v[p:p + 1, :], (SUB, n))

    for k in range(blocks):
        cols = [along_lanes(a[k], SUB * k + p) for p in range(SUB)]
        e = {(i, p): along_sublanes(cols[p], i) for p in range(SUB) for i in range(p, SUB)}
        r, l = [], {}
        for p in range(SUB):
            r.append(lax.rsqrt(e[p, p]))
            for i in range(p + 1, SUB):
                l[i, p] = e[i, p] * r[p]
            for q in range(p + 1, SUB):
                for i in range(q, SUB):
                    e[i, q] = e[i, q] - l[i, p] * l[q, p]

        def forward(values):
            out = []
            for p in range(SUB):
                v = values[p]
                for q in range(p):
                    v = v - l[p, q] * out[q]
                out.append(v * r[p])
            return out

        upper = forward([along_sublanes(a[k], p) for p in range(SUB)])
        inverse = forward([along_sublanes(j[k], p) for p in range(SUB)])
        rows.extend(v[:1] for v in inverse)
        for i in range(k + 1, blocks):
            lower = forward([along_lanes(a[i], SUB * k + p) for p in range(SUB)])
            for p in range(SUB):
                a[i] = a[i] - lower[p] * upper[p]
                j[i] = j[i] - lower[p] * inverse[p]
    return rows


def tucker_kernel(nv, x_hbm, start_hbm, y_ref, factor_hbm, xbuf, start_ref, factor_ref, rawbox, rawin, g_ref, basis_ref, block_ref, last_ref, product_ref, outbox, s_ref, mine,
                  theirs, inbox, total, parts, zparts, load_sem, swap_sem, rs_send, rs_recv, z_send, z_recv, ag_send, ag_recv,
                  back_sem, out_send, out_recv, keep_sem, side_sem, raw_send, raw_recv):
    wide = lax.axis_index("wide")
    y = lax.axis_index("slab")
    core = wide % CORES
    x = (wide // CORES) % XS
    z = wide // (CORES * XS)
    me = x * YS + y
    sibling = (wide + 1 - 2 * core, y)
    groups = range(len(GROUPS))

    def plane_device(p):
        return ((z * XS + p // YS) * CORES + core, p % YS)

    def z_device(q):
        return ((q * XS + x) * CORES + core, y)

    barrier = pltpu.get_barrier_semaphore()
    pl.semaphore_signal(barrier, inc=1, device_id=sibling, device_id_type=MESH)

    @pl.loop(1, PLANE)
    def _(d):
        pl.semaphore_signal(barrier, inc=1, device_id=plane_device((me + d) % PLANE), device_id_type=MESH)

    @pl.loop(1, ZS)
    def _(d):
        pl.semaphore_signal(barrier, inc=1, device_id=z_device((z + d) % ZS), device_id_type=MESH)

    rows = x_hbm.shape[0]
    steps = rows // CHUNK

    def load(c):
        return pltpu.make_async_copy(x_hbm.at[pl.ds(c * CHUNK, CHUNK)], xbuf.at[pl.ds(c * CHUNK, CHUNK)], load_sem.at[c])

    for c in range(steps):
        load(c).start()
    load_start = pltpu.make_async_copy(start_hbm, start_ref, side_sem.at[0])
    load_start.start()
    s_ref[...] = jnp.zeros_like(s_ref)

    @pl.loop(0, steps)
    def _(c):
        load(c).wait()
        value = xbuf[pl.ds(pl.multiple_of(c * CHUNK, CHUNK), CHUNK), :]
        high = value.astype(jnp.bfloat16)
        low = (value - high.astype(jnp.float32)).astype(jnp.bfloat16)
        s_ref[...] += 0.5 * lax.dot_general(high, high, TN, preferred_element_type=jnp.float32) + lax.dot_general(
            high, low, TN, preferred_element_type=jnp.float32)

    load_start.wait()
    basis_ref[...] = start_ref[...].T
    width = 2 * YS
    count = CHUNK // width
    pairs = CHUNK // YS
    halves = steps // nv

    def sort_raw(r):
        for k in range(N1 // TILE):
            product_ref[...] = xbuf[r * CHUNK:(r + 1) * CHUNK, k * TILE:(k + 1) * TILE]
            for p in range(YS):
                for i in range(2):
                    rawbox[r, p, k, pl.ds(i, count, stride=2), :] = product_ref[pl.ds(2 * p + i, count, stride=width), :]

    def raw(r, p, source):
        return pltpu.make_async_remote_copy(
            rawbox.at[r, p], rawin.at[r, source], raw_send.at[r, p], raw_recv.at[r, source], device_id=(wide, p), device_id_type=MESH)

    def send_raw(r):
        for d in (2, 1, 3):
            raw(r, (y + d) % YS, y).start()

    scale = 1.0 / (rows * PLANE * ZS * CORES)
    pl.semaphore_wait(barrier, PLANE + ZS - 1)

    def block(n):
        i, j = PAIRS[n]
        a = s_ref[i * TILE:(i + 1) * TILE, j * TILE:(j + 1) * TILE]
        b = s_ref[j * TILE:(j + 1) * TILE, i * TILE:(i + 1) * TILE]
        return (a + b.T) * scale

    def span(g):
        first, last = GROUPS[g]
        return pl.ds(first * TILE, (last - first) * TILE)

    def share(g):
        first, last = GROUPS[g]
        return pl.ds(first * OWN, (last - first) * OWN)

    def owned(g, p):
        first, last = GROUPS[g]
        return pl.ds(pl.multiple_of(first * TILE + p * ((last - first) * OWN), SUB), (last - first) * OWN)

    def swap(g):
        return pltpu.make_async_remote_copy(
            theirs.at[span(g)], inbox.at[span(g)], swap_sem.at[0, g], swap_sem.at[1, g], device_id=sibling, device_id_type=MESH)

    for g in groups:
        for c in range(CORES):
            @pl.when(core == c)
            def _():
                for n in range(*GROUPS[g]):
                    theirs[n * TILE:(n + 1) * TILE, :] = block((1 - c) * HALF + n)
        swap(g).start()
    for c in range(CORES):
        @pl.when(core == c)
        def _():
            for n in range(HALF):
                mine[n * TILE:(n + 1) * TILE, :] = block(c * HALF + n)
    for r in range(RAW):
        sort_raw(r)

    def scatter(g, p, source):
        return pltpu.make_async_remote_copy(
            mine.at[owned(g, p)], parts.at[source, share(g)], rs_send.at[g, p], rs_recv.at[g, source],
            device_id=plane_device(p), device_id_type=MESH)

    def along_z(g, q, source):
        return pltpu.make_async_remote_copy(
            zparts.at[source, share(g)], zparts.at[source, share(g)], z_send.at[g, q], z_recv.at[g, source],
            device_id=z_device(q), device_id_type=MESH)

    done = total.at[core]

    def gather(g, p, source):
        return pltpu.make_async_remote_copy(
            done.at[owned(g, source)], done.at[owned(g, source)], ag_send.at[g, p], ag_recv.at[g, source],
            device_id=plane_device(p), device_id_type=MESH)

    def back(g, c):
        return pltpu.make_async_remote_copy(
            total.at[c, span(g)], total.at[c, span(g)], back_sem.at[0, g], back_sem.at[1, g], device_id=sibling, device_id_type=MESH)

    for g in groups:
        swap(g).wait_recv()
        mine[span(g), :] += inbox[span(g), :]

        @pl.loop(1, PLANE)
        def _(d):
            scatter(g, (me + d) % PLANE, me).start()

    for g in groups:
        zparts[z, share(g), :] = mine[owned(g, me), :]

        @pl.loop(1, PLANE)
        def _(d):
            source = (me + PLANE - d) % PLANE
            scatter(g, (me + d) % PLANE, source).wait_recv()
            zparts[z, share(g), :] += parts[source, share(g), :]

        @pl.loop(1, ZS)
        def _(d):
            along_z(g, (z + d) % ZS, z).start()

    send_raw(0)

    for g in groups:
        @pl.loop(1, ZS)
        def _(d):
            along_z(g, (z + d) % ZS, (z + ZS - d) % ZS).wait_recv()

        value = zparts[0, share(g), :]
        for q in range(1, ZS):
            value = value + zparts[q, share(g), :]
        done[owned(g, me), :] = value

        @pl.loop(1, PLANE)
        def _(d):
            gather(g, (me + d) % PLANE, me).start()

    for g in groups:
        @pl.loop(1, PLANE)
        def _(d):
            gather(g, (me + d) % PLANE, (me + PLANE - d) % PLANE).wait_recv()

        back(g, core).start()

    for r in range(1, RAW):
        send_raw(r)

    for g in groups:
        back(g, 1 - core).wait_recv()
        for half in range(CORES):
            for m in range(*GROUPS[g]):
                i, j = PAIRS[half * HALF + m]
                value = total[half, m * TILE:(m + 1) * TILE, :]
                g_ref[i * TILE:(i + 1) * TILE, j * TILE:(j + 1) * TILE] = value
                if i != j:
                    g_ref[j * TILE:(j + 1) * TILE, i * TILE:(i + 1) * TILE] = value.T

    def times(a, b, dims):
        return lax.dot_general(a, b, dims, precision=HIGHEST, preferred_element_type=jnp.float32)

    def inverse_triangle(block_):
        for n, row in enumerate(inverse_factor(times(block_, block_, NT), RANK)):
            s_ref[n:n + 1, :RANK] = row
        return s_ref[:RANK, :RANK]

    @pl.loop(0, SWEEPS - 2)
    def _(sweep):
        block_ref[...] = times(basis_ref[...], g_ref[...], NN)
        basis_ref[...] = times(inverse_triangle(block_ref[...]), block_ref[...], NN)

    block_ref[...] = times(basis_ref[...], g_ref[...], NN)
    last_ref[...] = times(block_ref[...], g_ref[...], NN)
    def place(c, source):
        return y_ref.at[c // halves, pl.ds((source * halves + c % halves) * pairs, pairs)]

    def send(c, p, source):
        return pltpu.make_async_remote_copy(
            outbox.at[p, pl.ds(c * pairs, pairs)], place(c, source), out_send.at[c, p], out_recv.at[c, source],
            device_id=(wide, p), device_id_type=MESH)

    def arrived(r, source):
        return pltpu.make_async_copy(outbox.at[source, pl.ds(r * pairs, pairs)], place(r, source), out_recv.at[r, source])

    def keep(c):
        return pltpu.make_async_copy(outbox.at[y, pl.ds(c * pairs, pairs)], place(c, y), keep_sem.at[c])

    @pl.loop(RAW, steps)
    def _(c):
        product_ref[...] = times(xbuf[pl.ds(pl.multiple_of(c * CHUNK, CHUNK), CHUNK), :], last_ref[...], NT)
        for p in range(YS):
            for i in range(2):
                outbox[p, pl.ds(c * pairs + i, count, stride=2), :] = product_ref[pl.ds(2 * p + i, count, stride=width), :]
        for d in (2, 1, 3):
            send(c, (y + d) % YS, y).start()
        keep(c).start()

    for r in range(RAW):
        rawin[r, y] = rawbox[r, y]
        for d in (2, 1, 3):
            raw(r, (y + d) % YS, (y + YS - d) % YS).wait_recv()
        for source in range(YS):
            outbox[source, r * pairs:(r + 1) * pairs, :] = times(
                jnp.concatenate([rawin[r, source, k] for k in range(N1 // TILE)], axis=1), last_ref[...], NT)
            arrived(r, source).start()

    factor_ref[...] = jnp.zeros_like(factor_ref)

    @pl.loop(0, 2)
    def _(sweep):
        inverse = inverse_triangle(block_ref[...])

        @pl.when(sweep == 0)
        def _():
            factor_ref[...] = inverse
            block_ref[...] = times(inverse, last_ref[...], NN)

        @pl.when(sweep == 1)
        def _():
            factor_ref[...] = times(inverse, factor_ref[...], NN)

    for g in groups:
        swap(g).wait_send()
        back(g, core).wait_send()

        @pl.loop(1, PLANE)
        def _(d):
            p = (me + d) % PLANE
            scatter(g, p, me).wait_send()
            gather(g, p, me).wait_send()

        @pl.loop(1, ZS)
        def _(d):
            along_z(g, (z + d) % ZS, z).wait_send()

    store_factor = pltpu.make_async_copy(factor_ref, factor_hbm, side_sem.at[1])
    store_factor.start()
    for r in range(RAW):
        for d in (2, 1, 3):
            raw(r, (y + d) % YS, y).wait_send()
        for source in range(YS):
            arrived(r, source).wait()

    @pl.loop(RAW, steps)
    def _(c):
        keep(c).wait()
        for d in (2, 1, 3):
            send(c, (y + d) % YS, y).wait_send()
            send(c, (y + d) % YS, (y + YS - d) % YS).wait_recv()

    store_factor.wait()


def three(value):
    high = value.astype(jnp.bfloat16)
    rest = value - high.astype(jnp.float32)
    middle = rest.astype(jnp.bfloat16)
    return high, middle, (rest - middle.astype(jnp.float32)).astype(jnp.bfloat16)


def finish_kernel(y_hbm, factor_hbm, out_hbm, y_ref, factor_ref, out_ref, sem, factor_sem):
    steps, rows = y_ref.shape[:2]

    def load(c):
        return pltpu.make_async_copy(y_hbm.at[c], y_ref.at[c], sem.at[0, c])

    def store(c):
        return pltpu.make_async_copy(out_ref.at[c], out_hbm.at[c], sem.at[1, c])

    load_factor = pltpu.make_async_copy(factor_hbm, factor_ref, factor_sem)
    load_factor.start()
    for c in range(steps):
        load(c).start()
    load_factor.wait()
    high, middle, low = three(factor_ref[...])
    stacked = jnp.concatenate([jnp.concatenate([high, middle], axis=0)] * 2, axis=1)
    rest = jnp.concatenate([low, high], axis=1)

    @pl.loop(0, steps)
    def _(c):
        load(c).wait()
        high, middle, low = three(y_ref[c])
        first = lax.dot_general(
            jnp.concatenate([high, middle], axis=1), stacked, NT, preferred_element_type=jnp.float32)
        second = lax.dot_general(jnp.concatenate([high, low], axis=1), rest, NT, preferred_element_type=jnp.float32)
        out_ref[c] = first[:, :RANK] + (first[:, RANK:] + second)
        store(c).start()

    @pl.loop(0, steps)
    def _(c):
        store(c).wait()


def per_device(fields, start_basis):
    nv, n2, n3, n1 = fields.shape
    unfolded = fields.reshape(-1, n1)
    rows = unfolded.shape[0]
    steps = rows // CHUNK
    stages = len(GROUPS)
    y, factor = pl.pallas_call(
        functools.partial(tucker_kernel, nv),
        out_shape=[jax.ShapeDtypeStruct((nv, rows // nv, RANK), jnp.float32), jax.ShapeDtypeStruct((RANK, RANK), jnp.float32)],
        in_specs=[pl.BlockSpec(memory_space=pltpu.HBM)] * 2,
        out_specs=[pl.BlockSpec(memory_space=pltpu.HBM)] * 2,
        scratch_shapes=[
            pltpu.VMEM((rows, n1), jnp.float32),
            pltpu.VMEM((n1, RANK), jnp.float32),
            pltpu.VMEM((RANK, RANK), jnp.float32),
            pltpu.VMEM((RAW, YS, n1 // TILE, CHUNK // YS, TILE), jnp.float32),
            pltpu.VMEM((RAW, YS, n1 // TILE, CHUNK // YS, TILE), jnp.float32),
            pltpu.VMEM((n1, n1), jnp.float32),
            pltpu.VMEM((RANK, n1), jnp.float32),
            pltpu.VMEM((RANK, n1), jnp.float32),
            pltpu.VMEM((RANK, n1), jnp.float32),
            pltpu.VMEM((CHUNK, RANK), jnp.float32),
            pltpu.VMEM((YS, rows // YS, RANK), jnp.float32),
            pltpu.VMEM((n1, n1), jnp.float32),
            pltpu.VMEM((HALF * TILE, TILE), jnp.float32),
            pltpu.VMEM((HALF * TILE, TILE), jnp.float32),
            pltpu.VMEM((HALF * TILE, TILE), jnp.float32),
            pltpu.VMEM((CORES, HALF * TILE, TILE), jnp.float32),
            pltpu.VMEM((PLANE, HALF * OWN, TILE), jnp.float32),
            pltpu.VMEM((ZS, HALF * OWN, TILE), jnp.float32),
            pltpu.SemaphoreType.DMA((steps,)),
            pltpu.SemaphoreType.DMA((2, stages)),
            pltpu.SemaphoreType.DMA((stages, PLANE)),
            pltpu.SemaphoreType.DMA((stages, PLANE)),
            pltpu.SemaphoreType.DMA((stages, ZS)),
            pltpu.SemaphoreType.DMA((stages, ZS)),
            pltpu.SemaphoreType.DMA((stages, PLANE)),
            pltpu.SemaphoreType.DMA((stages, PLANE)),
            pltpu.SemaphoreType.DMA((2, stages)),
            pltpu.SemaphoreType.DMA((steps, YS)),
            pltpu.SemaphoreType.DMA((steps, YS)),
            pltpu.SemaphoreType.DMA((steps,)),
            pltpu.SemaphoreType.DMA((2,)),
            pltpu.SemaphoreType.DMA((RAW, YS)),
            pltpu.SemaphoreType.DMA((RAW, YS)),
        ],
        compiler_params=pltpu.CompilerParams(collective_id=0, has_side_effects=True, vmem_limit_bytes=67043328),
    )(unfolded, start_basis)
    parts = (steps, CHUNK, RANK)
    out = pl.pallas_call(
        finish_kernel,
        out_shape=jax.ShapeDtypeStruct(parts, jnp.float32),
        in_specs=[pl.BlockSpec(memory_space=pltpu.HBM)] * 2,
        out_specs=pl.BlockSpec(memory_space=pltpu.HBM),
        scratch_shapes=[
            pltpu.VMEM(parts, jnp.float32),
            pltpu.VMEM((RANK, RANK), jnp.float32),
            pltpu.VMEM(parts, jnp.float32),
            pltpu.SemaphoreType.DMA((2, steps)),
            pltpu.SemaphoreType.DMA,
        ],
    )(y.reshape(parts), factor)
    return out.reshape(nv, n2 * YS, n3 // YS, RANK)


def solution(mesh):
    in_specs = (P(None, "slab", "wide", None), P())
    out_specs = P(None, None, ("wide", "slab"), None)
    return jax.shard_map(
        per_device, mesh=mesh, in_specs=in_specs, out_specs=out_specs, check_vma=False
    )
```

```python
import functools

import jax
import jax.numpy as jnp
from jax import lax
from jax.experimental import pallas as pl
from jax.experimental.pallas import tpu as pltpu
from jax.sharding import PartitionSpec as P

SWEEPS = 4
MESH = pl.DeviceIdType.MESH
CORES, XS, ZS, YS = 2, 4, 8, 4
PLANE = XS * YS
N1 = 512
TILE = 128
PAIRS = [(i, j) for i in range(N1 // TILE) for j in range(i, N1 // TILE)]
HALF = len(PAIRS) // CORES
OWN = TILE // PLANE
GROUPS = ((0, 3), (3, HALF))
CHUNK = 512
SUB = 8
RAW = 2
Z_STEPS = (1, -1, -3, 3)
Z_SOURCE = (0, 0, 3, 4)
Z_TARGET = (1, 2, 5, 6)
RANK = 128
HIGHEST = lax.Precision.HIGHEST
NT = (((1,), (1,)), ((), ()))
TN = (((0,), (0,)), ((), ()))
NN = (((1,), (0,)), ((), ()))


def inverse_factor(square, n):
    blocks = n // SUB
    lane = lax.broadcasted_iota(jnp.int32, (SUB, n), 1)
    sub = lax.broadcasted_iota(jnp.int32, (SUB, n), 0)
    a = [square[SUB * i:SUB * (i + 1), :] for i in range(blocks)]
    j = [(lane == sub + SUB * i).astype(jnp.float32) for i in range(blocks)]
    rows = []

    def along_lanes(v, c):
        return jnp.broadcast_to(v[:, c:c + 1], (SUB, n))

    def along_sublanes(v, p):
        return jnp.broadcast_to(v[p:p + 1, :], (SUB, n))

    for k in range(blocks):
        cols = [along_lanes(a[k], SUB * k + p) for p in range(SUB)]
        e = {(i, p): along_sublanes(cols[p], i) for p in range(SUB) for i in range(p, SUB)}
        r, l = [], {}
        for p in range(SUB):
            r.append(lax.rsqrt(e[p, p]))
            for i in range(p + 1, SUB):
                l[i, p] = e[i, p] * r[p]
            for q in range(p + 1, SUB):
                for i in range(q, SUB):
                    e[i, q] = e[i, q] - l[i, p] * l[q, p]

        def forward(values):
            out = []
            for p in range(SUB):
                v = values[p]
                for q in range(p):
                    v = v - l[p, q] * out[q]
                out.append(v * r[p])
            return out

        upper = forward([along_sublanes(a[k], p) for p in range(SUB)])
        inverse = forward([along_sublanes(j[k], p) for p in range(SUB)])
        rows.extend(v[:1] for v in inverse)
        for i in range(k + 1, blocks):
            lower = forward([along_lanes(a[i], SUB * k + p) for p in range(SUB)])
            for p in range(SUB):
                a[i] = a[i] - lower[p] * upper[p]
                j[i] = j[i] - lower[p] * inverse[p]
    return rows


def three(value):
    high = value.astype(jnp.bfloat16)
    rest = value - high.astype(jnp.float32)
    middle = rest.astype(jnp.bfloat16)
    return high, middle, (rest - middle.astype(jnp.float32)).astype(jnp.bfloat16)


def tucker_kernel(nv, x_hbm, start_hbm, out_hbm, xbuf, y_ref, out_ref, start_ref, factor_ref, rawbox, rawin, g_ref, basis_ref, block_ref, last_ref, product_ref, outbox, s_ref, mine,
                  theirs, inbox, total, parts, zparts, load_sem, swap_sem, rs_send, rs_recv, z_send, z_recv, ag_send, ag_recv,
                  back_sem, out_send, out_recv, store_sem, side_sem, raw_send, raw_recv):
    wide = lax.axis_index("wide")
    y = lax.axis_index("slab")
    core = wide % CORES
    x = (wide // CORES) % XS
    z = wide // (CORES * XS)
    me = x * YS + y
    sibling = (wide + 1 - 2 * core, y)
    groups = range(len(GROUPS))

    def plane_device(p):
        return ((z * XS + p // YS) * CORES + core, p % YS)

    def z_device(q):
        return ((q * XS + x) * CORES + core, y)

    barrier = pltpu.get_barrier_semaphore()
    pl.semaphore_signal(barrier, inc=1, device_id=sibling, device_id_type=MESH)

    @pl.loop(1, PLANE)
    def _(d):
        pl.semaphore_signal(barrier, inc=1, device_id=plane_device((me + d) % PLANE), device_id_type=MESH)

    for step in Z_STEPS:
        pl.semaphore_signal(barrier, inc=1, device_id=z_device((z + ZS + step) % ZS), device_id_type=MESH)

    rows = x_hbm.shape[0]
    steps = rows // CHUNK

    def load(c):
        return pltpu.make_async_copy(x_hbm.at[pl.ds(c * CHUNK, CHUNK)], xbuf.at[pl.ds(c * CHUNK, CHUNK)], load_sem.at[c])

    for c in range(steps):
        load(c).start()
    load_start = pltpu.make_async_copy(start_hbm, start_ref, side_sem.at[0])
    load_start.start()
    s_ref[...] = jnp.zeros_like(s_ref)

    @pl.loop(0, steps)
    def _(c):
        load(c).wait()
        value = xbuf[pl.ds(pl.multiple_of(c * CHUNK, CHUNK), CHUNK), :]
        high = value.astype(jnp.bfloat16)
        low = (value - high.astype(jnp.float32)).astype(jnp.bfloat16)
        s_ref[...] += 0.5 * lax.dot_general(high, high, TN, preferred_element_type=jnp.float32) + lax.dot_general(
            high, low, TN, preferred_element_type=jnp.float32)

    load_start.wait()
    basis_ref[...] = start_ref[...].T
    width = 2 * YS
    count = CHUNK // width
    pairs = CHUNK // YS
    halves = steps // nv

    def sort_raw(r):
        for k in range(N1 // TILE):
            product_ref[...] = xbuf[r * CHUNK:(r + 1) * CHUNK, k * TILE:(k + 1) * TILE]
            for p in range(YS):
                for i in range(2):
                    rawbox[r, p, k, pl.ds(i, count, stride=2), :] = product_ref[pl.ds(2 * p + i, count, stride=width), :]

    def raw(r, p, source):
        return pltpu.make_async_remote_copy(
            rawbox.at[r, p], rawin.at[r, source], raw_send.at[r, p], raw_recv.at[r, source], device_id=(wide, p), device_id_type=MESH)

    def send_raw(r):
        for d in (2, 1, 3):
            raw(r, (y + d) % YS, y).start()

    scale = 1.0 / (rows * PLANE * ZS * CORES)
    pl.semaphore_wait(barrier, PLANE + len(Z_STEPS))

    def block(n):
        i, j = PAIRS[n]
        a = s_ref[i * TILE:(i + 1) * TILE, j * TILE:(j + 1) * TILE]
        b = s_ref[j * TILE:(j + 1) * TILE, i * TILE:(i + 1) * TILE]
        return (a + b.T) * scale

    def span(g):
        first, last = GROUPS[g]
        return pl.ds(first * TILE, (last - first) * TILE)

    def share(g):
        first, last = GROUPS[g]
        return pl.ds(first * OWN, (last - first) * OWN)

    def owned(g, p):
        first, last = GROUPS[g]
        return pl.ds(pl.multiple_of(first * TILE + p * ((last - first) * OWN), SUB), (last - first) * OWN)

    def swap(g):
        return pltpu.make_async_remote_copy(
            theirs.at[span(g)], inbox.at[span(g)], swap_sem.at[0, g], swap_sem.at[1, g], device_id=sibling, device_id_type=MESH)

    for g in groups:
        for c in range(CORES):
            @pl.when(core == c)
            def _():
                for n in range(*GROUPS[g]):
                    theirs[n * TILE:(n + 1) * TILE, :] = block((1 - c) * HALF + n)
        swap(g).start()
    for c in range(CORES):
        @pl.when(core == c)
        def _():
            for n in range(HALF):
                mine[n * TILE:(n + 1) * TILE, :] = block(c * HALF + n)
    for r in range(RAW):
        sort_raw(r)

    def scatter(g, p, source):
        return pltpu.make_async_remote_copy(
            mine.at[owned(g, p)], parts.at[source, share(g)], rs_send.at[g, p], rs_recv.at[g, source],
            device_id=plane_device(p), device_id_type=MESH)

    def along_z(g, n):
        return pltpu.make_async_remote_copy(
            zparts.at[Z_SOURCE[n], share(g)], zparts.at[Z_TARGET[n], share(g)], z_send.at[g, n], z_recv.at[g, n],
            device_id=z_device((z + ZS + Z_STEPS[n]) % ZS), device_id_type=MESH)

    done = total.at[core]

    def gather(g, p, source):
        return pltpu.make_async_remote_copy(
            done.at[owned(g, source)], done.at[owned(g, source)], ag_send.at[g, p], ag_recv.at[g, source],
            device_id=plane_device(p), device_id_type=MESH)

    def back(g, c):
        return pltpu.make_async_remote_copy(
            total.at[c, span(g)], total.at[c, span(g)], back_sem.at[0, g], back_sem.at[1, g], device_id=sibling, device_id_type=MESH)

    for g in groups:
        swap(g).wait_recv()
        mine[span(g), :] += inbox[span(g), :]

        @pl.loop(1, PLANE)
        def _(d):
            scatter(g, (me + d) % PLANE, me).start()

    for g in groups:
        zparts[0, share(g), :] = mine[owned(g, me), :]

        @pl.loop(1, PLANE)
        def _(d):
            source = (me + PLANE - d) % PLANE
            scatter(g, (me + d) % PLANE, source).wait_recv()
            zparts[0, share(g), :] += parts[source, share(g), :]

        for n in (0, 1):
            along_z(g, n).start()

    send_raw(0)

    for g in groups:
        for n in (0, 1):
            along_z(g, n).wait_recv()
        two = zparts[0, share(g), :] + zparts[2, share(g), :]
        zparts[4, share(g), :] = two
        zparts[3, share(g), :] = two + zparts[1, share(g), :]
        for n in (2, 3):
            along_z(g, n).start()

    for g in groups:
        for n in (2, 3):
            along_z(g, n).wait_recv()
        value = zparts[3, share(g), :] + (zparts[5, share(g), :] + zparts[6, share(g), :])
        done[owned(g, me), :] = value

        @pl.loop(1, PLANE)
        def _(d):
            gather(g, (me + d) % PLANE, me).start()

    for g in groups:
        @pl.loop(1, PLANE)
        def _(d):
            gather(g, (me + d) % PLANE, (me + PLANE - d) % PLANE).wait_recv()

        back(g, core).start()

    for r in range(1, RAW):
        send_raw(r)

    for g in groups:
        back(g, 1 - core).wait_recv()
        for half in range(CORES):
            for m in range(*GROUPS[g]):
                i, j = PAIRS[half * HALF + m]
                value = total[half, m * TILE:(m + 1) * TILE, :]
                g_ref[i * TILE:(i + 1) * TILE, j * TILE:(j + 1) * TILE] = value
                if i != j:
                    g_ref[j * TILE:(j + 1) * TILE, i * TILE:(i + 1) * TILE] = value.T

    def times(a, b, dims):
        return lax.dot_general(a, b, dims, precision=HIGHEST, preferred_element_type=jnp.float32)

    def inverse_triangle(block_):
        for n, row in enumerate(inverse_factor(times(block_, block_, NT), RANK)):
            s_ref[n:n + 1, :RANK] = row
        return s_ref[:RANK, :RANK]

    @pl.loop(0, SWEEPS - 2)
    def _(sweep):
        block_ref[...] = times(basis_ref[...], g_ref[...], NN)
        basis_ref[...] = times(inverse_triangle(block_ref[...]), block_ref[...], NN)

    block_ref[...] = times(basis_ref[...], g_ref[...], NN)
    last_ref[...] = times(block_ref[...], g_ref[...], NN)
    def place(c, source):
        return y_ref.at[c // halves, pl.ds((source * halves + c % halves) * pairs, pairs)]

    def send(c, p, source):
        return pltpu.make_async_remote_copy(
            outbox.at[p, pl.ds(c * pairs, pairs)], place(c, source), out_send.at[c, p], out_recv.at[c, source],
            device_id=(wide, p), device_id_type=MESH)

    @pl.loop(RAW, steps)
    def _(c):
        product_ref[...] = times(xbuf[pl.ds(pl.multiple_of(c * CHUNK, CHUNK), CHUNK), :], last_ref[...], NT)
        for p in range(YS):
            for i in range(2):
                outbox[p, pl.ds(c * pairs + i, count, stride=2), :] = product_ref[pl.ds(2 * p + i, count, stride=width), :]
        for d in (2, 1, 3):
            send(c, (y + d) % YS, y).start()
        y_ref[c // halves, pl.ds(pl.multiple_of((y * halves + c % halves) * pairs, pairs), pairs), :] = outbox[
            y, pl.ds(pl.multiple_of(c * pairs, pairs), pairs), :]

    for r in range(RAW):
        rawin[r, y] = rawbox[r, y]
        for d in (2, 1, 3):
            raw(r, (y + d) % YS, (y + YS - d) % YS).wait_recv()
        for source in range(YS):
            first = (source * halves + r % halves) * pairs
            y_ref[r // halves, first:first + pairs, :] = times(
                jnp.concatenate([rawin[r, source, k] for k in range(N1 // TILE)], axis=1), last_ref[...], NT)

    factor_ref[...] = jnp.zeros_like(factor_ref)

    @pl.loop(0, 2)
    def _(sweep):
        inverse = inverse_triangle(block_ref[...])

        @pl.when(sweep == 0)
        def _():
            factor_ref[...] = inverse
            block_ref[...] = times(inverse, last_ref[...], NN)

        @pl.when(sweep == 1)
        def _():
            factor_ref[...] = times(inverse, factor_ref[...], NN)

    for g in groups:
        swap(g).wait_send()
        back(g, core).wait_send()

        @pl.loop(1, PLANE)
        def _(d):
            p = (me + d) % PLANE
            scatter(g, p, me).wait_send()
            gather(g, p, me).wait_send()

        for n in range(len(Z_STEPS)):
            along_z(g, n).wait_send()

    high, middle, low = three(factor_ref[...])
    stacked = jnp.concatenate([jnp.concatenate([high, middle], axis=0)] * 2, axis=1)
    rest = jnp.concatenate([low, high], axis=1)

    def part(c, source):
        return pl.ds(pl.multiple_of((source * halves + c % halves) * pairs, pairs), pairs)

    def store(c, source):
        return pltpu.make_async_copy(
            out_ref.at[c // halves, part(c, source)], out_hbm.at[c // halves, part(c, source)], store_sem.at[c, source])

    def finish(c):
        value = jnp.concatenate([y_ref[c // halves, part(c, source), :] for source in range(YS)], axis=0)
        high_, middle_, low_ = three(value)
        first = lax.dot_general(jnp.concatenate([high_, middle_], axis=1), stacked, NT, preferred_element_type=jnp.float32)
        second = lax.dot_general(jnp.concatenate([high_, low_], axis=1), rest, NT, preferred_element_type=jnp.float32)
        value = first[:, :RANK] + (first[:, RANK:] + second)
        for source in range(YS):
            out_ref[c // halves, part(c, source), :] = value[source * pairs:(source + 1) * pairs, :]
            store(c, source).start()

    @pl.loop(0, RAW)
    def _(r):
        finish(r)

    @pl.loop(RAW, steps)
    def _(c):
        for d in (2, 1, 3):
            send(c, (y + d) % YS, (y + YS - d) % YS).wait_recv()
        finish(c)

    for r in range(RAW):
        for d in (2, 1, 3):
            raw(r, (y + d) % YS, y).wait_send()

    @pl.loop(RAW, steps)
    def _(c):
        for d in (2, 1, 3):
            send(c, (y + d) % YS, y).wait_send()

    @pl.loop(0, steps)
    def _(c):
        for source in range(YS):
            store(c, source).wait()


def copy_kernel(y_hbm, out_hbm, y_ref, sem):
    steps = y_ref.shape[0]

    def load(c):
        return pltpu.make_async_copy(y_hbm.at[c], y_ref.at[c], sem.at[0, c])

    def store(c):
        return pltpu.make_async_copy(y_ref.at[c], out_hbm.at[c], sem.at[1, c])

    for c in range(steps):
        load(c).start()
    for c in range(steps):
        load(c).wait()
        store(c).start()
    for c in range(steps):
        store(c).wait()


def per_device(fields, start_basis):
    nv, n2, n3, n1 = fields.shape
    unfolded = fields.reshape(-1, n1)
    rows = unfolded.shape[0]
    steps = rows // CHUNK
    stages = len(GROUPS)
    y = pl.pallas_call(
        functools.partial(tucker_kernel, nv),
        out_shape=jax.ShapeDtypeStruct((nv, rows // nv, RANK), jnp.float32),
        in_specs=[pl.BlockSpec(memory_space=pltpu.HBM)] * 2,
        out_specs=pl.BlockSpec(memory_space=pltpu.HBM),
        scratch_shapes=[
            pltpu.VMEM((rows, n1), jnp.float32),
            pltpu.VMEM((nv, rows // nv, RANK), jnp.float32),
            pltpu.VMEM((nv, rows // nv, RANK), jnp.float32),
            pltpu.VMEM((n1, RANK), jnp.float32),
            pltpu.VMEM((RANK, RANK), jnp.float32),
            pltpu.VMEM((RAW, YS, n1 // TILE, CHUNK // YS, TILE), jnp.float32),
            pltpu.VMEM((RAW, YS, n1 // TILE, CHUNK // YS, TILE), jnp.float32),
            pltpu.VMEM((n1, n1), jnp.float32),
            pltpu.VMEM((RANK, n1), jnp.float32),
            pltpu.VMEM((RANK, n1), jnp.float32),
            pltpu.VMEM((RANK, n1), jnp.float32),
            pltpu.VMEM((CHUNK, RANK), jnp.float32),
            pltpu.VMEM((YS, rows // YS, RANK), jnp.float32),
            pltpu.VMEM((n1, n1), jnp.float32),
            pltpu.VMEM((HALF * TILE, TILE), jnp.float32),
            pltpu.VMEM((HALF * TILE, TILE), jnp.float32),
            pltpu.VMEM((HALF * TILE, TILE), jnp.float32),
            pltpu.VMEM((CORES, HALF * TILE, TILE), jnp.float32),
            pltpu.VMEM((PLANE, HALF * OWN, TILE), jnp.float32),
            pltpu.VMEM((7, HALF * OWN, TILE), jnp.float32),
            pltpu.SemaphoreType.DMA((steps,)),
            pltpu.SemaphoreType.DMA((2, stages)),
            pltpu.SemaphoreType.DMA((stages, PLANE)),
            pltpu.SemaphoreType.DMA((stages, PLANE)),
            pltpu.SemaphoreType.DMA((stages, len(Z_STEPS))),
            pltpu.SemaphoreType.DMA((stages, len(Z_STEPS))),
            pltpu.SemaphoreType.DMA((stages, PLANE)),
            pltpu.SemaphoreType.DMA((stages, PLANE)),
            pltpu.SemaphoreType.DMA((2, stages)),
            pltpu.SemaphoreType.DMA((steps, YS)),
            pltpu.SemaphoreType.DMA((steps, YS)),
            pltpu.SemaphoreType.DMA((steps, YS)),
            pltpu.SemaphoreType.DMA((1,)),
            pltpu.SemaphoreType.DMA((RAW, YS)),
            pltpu.SemaphoreType.DMA((RAW, YS)),
        ],
        compiler_params=pltpu.CompilerParams(collective_id=0, has_side_effects=True, vmem_limit_bytes=67043328),
    )(unfolded, start_basis)
    parts = (2, rows // 2, RANK)
    out = pl.pallas_call(
        copy_kernel,
        out_shape=jax.ShapeDtypeStruct(parts, jnp.float32),
        in_specs=[pl.BlockSpec(memory_space=pltpu.HBM)],
        out_specs=pl.BlockSpec(memory_space=pltpu.HBM),
        scratch_shapes=[pltpu.VMEM(parts, jnp.float32), pltpu.SemaphoreType.DMA((2, 2))],
    )(y.reshape(parts))
    return out.reshape(nv, n2 * YS, n3 // YS, RANK)


def solution(mesh):
    in_specs = (P(None, "slab", "wide", None), P())
    out_specs = P(None, None, ("wide", "slab"), None)
    return jax.shard_map(
        per_device, mesh=mesh, in_specs=in_specs, out_specs=out_specs, check_vma=False
    )
```

```python
import functools

import jax
import jax.numpy as jnp
from jax import lax
from jax.experimental import pallas as pl
from jax.experimental.pallas import tpu as pltpu
from jax.sharding import PartitionSpec as P

SWEEPS = 4
MESH = pl.DeviceIdType.MESH
CORES, XS, ZS, YS = 2, 4, 8, 4
PLANE = XS * YS
N1 = 512
TILE = 128
PAIRS = [(i, j) for i in range(N1 // TILE) for j in range(i, N1 // TILE)]
HALF = len(PAIRS) // CORES
OWN = TILE // PLANE
GROUPS = ((0, 3), (3, HALF))
CHUNK = 512
SUB = 8
RAW = 2
Z_STEPS = (1, -1, -3, 3)
Z_SOURCE = (0, 0, 3, 4)
Z_TARGET = (1, 2, 5, 6)
RANK = 128
HIGHEST = lax.Precision.HIGHEST
NT = (((1,), (1,)), ((), ()))
TN = (((0,), (0,)), ((), ()))
NN = (((1,), (0,)), ((), ()))


def inverse_factor(square, n):
    blocks = n // SUB
    lane = lax.broadcasted_iota(jnp.int32, (SUB, n), 1)
    sub = lax.broadcasted_iota(jnp.int32, (SUB, n), 0)
    a = [square[SUB * i:SUB * (i + 1), :] for i in range(blocks)]
    j = [(lane == sub + SUB * i).astype(jnp.float32) for i in range(blocks)]
    rows = []

    def along_lanes(v, c):
        return jnp.broadcast_to(v[:, c:c + 1], (SUB, n))

    def along_sublanes(v, p):
        return jnp.broadcast_to(v[p:p + 1, :], (SUB, n))

    for k in range(blocks):
        cols = [along_lanes(a[k], SUB * k + p) for p in range(SUB)]
        e = {(i, p): along_sublanes(cols[p], i) for p in range(SUB) for i in range(p, SUB)}
        r, l = [], {}
        for p in range(SUB):
            r.append(lax.rsqrt(e[p, p]))
            for i in range(p + 1, SUB):
                l[i, p] = e[i, p] * r[p]
            for q in range(p + 1, SUB):
                for i in range(q, SUB):
                    e[i, q] = e[i, q] - l[i, p] * l[q, p]

        def forward(values):
            out = []
            for p in range(SUB):
                v = values[p]
                for q in range(p):
                    v = v - l[p, q] * out[q]
                out.append(v * r[p])
            return out

        upper = forward([along_sublanes(a[k], p) for p in range(SUB)])
        inverse = forward([along_sublanes(j[k], p) for p in range(SUB)])
        rows.extend(v[:1] for v in inverse)
        for i in range(k + 1, blocks):
            lower = forward([along_lanes(a[i], SUB * k + p) for p in range(SUB)])
            for p in range(SUB):
                a[i] = a[i] - lower[p] * upper[p]
                j[i] = j[i] - lower[p] * inverse[p]
    return rows


def three(value):
    high = value.astype(jnp.bfloat16)
    rest = value - high.astype(jnp.float32)
    middle = rest.astype(jnp.bfloat16)
    return high, middle, (rest - middle.astype(jnp.float32)).astype(jnp.bfloat16)


def tucker_kernel(nv, x_hbm, start_hbm, out_hbm, xbuf, y_ref, out_ref, start_ref, factor_ref, rawbox, rawin, g_ref, basis_ref, block_ref, last_ref, wide_ref, deep_ref, product_ref, outbox, s_ref, mine,
                  theirs, inbox, total, parts, zparts, load_sem, swap_sem, rs_send, rs_recv, z_send, z_recv, ag_send, ag_recv,
                  back_sem, out_send, out_recv, store_sem, side_sem, raw_send, raw_recv):
    wide = lax.axis_index("wide")
    y = lax.axis_index("slab")
    core = wide % CORES
    x = (wide // CORES) % XS
    z = wide // (CORES * XS)
    me = x * YS + y
    sibling = (wide + 1 - 2 * core, y)
    groups = range(len(GROUPS))

    def plane_device(p):
        return ((z * XS + p // YS) * CORES + core, p % YS)

    def z_device(q):
        return ((q * XS + x) * CORES + core, y)

    barrier = pltpu.get_barrier_semaphore()
    pl.semaphore_signal(barrier, inc=1, device_id=sibling, device_id_type=MESH)

    @pl.loop(1, PLANE)
    def _(d):
        pl.semaphore_signal(barrier, inc=1, device_id=plane_device((me + d) % PLANE), device_id_type=MESH)

    for step in Z_STEPS:
        pl.semaphore_signal(barrier, inc=1, device_id=z_device((z + ZS + step) % ZS), device_id_type=MESH)

    rows = x_hbm.shape[0]
    steps = rows // CHUNK

    def load(c):
        return pltpu.make_async_copy(x_hbm.at[pl.ds(c * CHUNK, CHUNK)], xbuf.at[pl.ds(c * CHUNK, CHUNK)], load_sem.at[c])

    for c in range(steps):
        load(c).start()
    load_start = pltpu.make_async_copy(start_hbm, start_ref, side_sem.at[0])
    load_start.start()
    s_ref[...] = jnp.zeros_like(s_ref)

    @pl.loop(0, steps)
    def _(c):
        load(c).wait()
        value = xbuf[pl.ds(pl.multiple_of(c * CHUNK, CHUNK), CHUNK), :]
        high = value.astype(jnp.bfloat16)
        low = (value - high.astype(jnp.float32)).astype(jnp.bfloat16)
        s_ref[...] += 0.5 * lax.dot_general(high, high, TN, preferred_element_type=jnp.float32) + lax.dot_general(
            high, low, TN, preferred_element_type=jnp.float32)

    load_start.wait()
    basis_ref[...] = start_ref[...].T
    width = 2 * YS
    count = CHUNK // width
    pairs = CHUNK // YS
    halves = steps // nv

    def sort_raw(r):
        for k in range(N1 // TILE):
            product_ref[...] = xbuf[r * CHUNK:(r + 1) * CHUNK, k * TILE:(k + 1) * TILE]
            for p in range(YS):
                for i in range(2):
                    rawbox[r, p, k, pl.ds(i, count, stride=2), :] = product_ref[pl.ds(2 * p + i, count, stride=width), :]

    def raw(r, p, source):
        return pltpu.make_async_remote_copy(
            rawbox.at[r, p], rawin.at[r, source], raw_send.at[r, p], raw_recv.at[r, source], device_id=(wide, p), device_id_type=MESH)

    def send_raw(r):
        for d in (2, 1, 3):
            raw(r, (y + d) % YS, y).start()

    scale = 1.0 / (rows * PLANE * ZS * CORES)
    pl.semaphore_wait(barrier, PLANE + len(Z_STEPS))

    def block(n):
        i, j = PAIRS[n]
        a = s_ref[i * TILE:(i + 1) * TILE, j * TILE:(j + 1) * TILE]
        b = s_ref[j * TILE:(j + 1) * TILE, i * TILE:(i + 1) * TILE]
        return (a + b.T) * scale

    def span(g):
        first, last = GROUPS[g]
        return pl.ds(first * TILE, (last - first) * TILE)

    def share(g):
        first, last = GROUPS[g]
        return pl.ds(first * OWN, (last - first) * OWN)

    def owned(g, p):
        first, last = GROUPS[g]
        return pl.ds(pl.multiple_of(first * TILE + p * ((last - first) * OWN), SUB), (last - first) * OWN)

    def swap(g):
        return pltpu.make_async_remote_copy(
            theirs.at[span(g)], inbox.at[span(g)], swap_sem.at[0, g], swap_sem.at[1, g], device_id=sibling, device_id_type=MESH)

    for g in groups:
        for c in range(CORES):
            @pl.when(core == c)
            def _():
                for n in range(*GROUPS[g]):
                    theirs[n * TILE:(n + 1) * TILE, :] = block((1 - c) * HALF + n)
        swap(g).start()
    for c in range(CORES):
        @pl.when(core == c)
        def _():
            for n in range(HALF):
                mine[n * TILE:(n + 1) * TILE, :] = block(c * HALF + n)
    for r in range(RAW):
        sort_raw(r)

    def scatter(g, p, source):
        return pltpu.make_async_remote_copy(
            mine.at[owned(g, p)], parts.at[source, share(g)], rs_send.at[g, p], rs_recv.at[g, source],
            device_id=plane_device(p), device_id_type=MESH)

    def along_z(g, n):
        return pltpu.make_async_remote_copy(
            zparts.at[Z_SOURCE[n], share(g)], zparts.at[Z_TARGET[n], share(g)], z_send.at[g, n], z_recv.at[g, n],
            device_id=z_device((z + ZS + Z_STEPS[n]) % ZS), device_id_type=MESH)

    done = total.at[core]

    def gather(g, p, source):
        return pltpu.make_async_remote_copy(
            done.at[owned(g, source)], done.at[owned(g, source)], ag_send.at[g, p], ag_recv.at[g, source],
            device_id=plane_device(p), device_id_type=MESH)

    def back(g, c):
        return pltpu.make_async_remote_copy(
            total.at[c, span(g)], total.at[c, span(g)], back_sem.at[0, g], back_sem.at[1, g], device_id=sibling, device_id_type=MESH)

    for g in groups:
        swap(g).wait_recv()
        mine[span(g), :] += inbox[span(g), :]

        @pl.loop(1, PLANE)
        def _(d):
            scatter(g, (me + d) % PLANE, me).start()

    for g in groups:
        zparts[0, share(g), :] = mine[owned(g, me), :]

        @pl.loop(1, PLANE)
        def _(d):
            source = (me + PLANE - d) % PLANE
            scatter(g, (me + d) % PLANE, source).wait_recv()
            zparts[0, share(g), :] += parts[source, share(g), :]

        for n in (0, 1):
            along_z(g, n).start()

    send_raw(0)

    for g in groups:
        for n in (0, 1):
            along_z(g, n).wait_recv()
        two = zparts[0, share(g), :] + zparts[2, share(g), :]
        zparts[4, share(g), :] = two
        zparts[3, share(g), :] = two + zparts[1, share(g), :]
        for n in (2, 3):
            along_z(g, n).start()

    for g in groups:
        for n in (2, 3):
            along_z(g, n).wait_recv()
        value = zparts[3, share(g), :] + (zparts[5, share(g), :] + zparts[6, share(g), :])
        done[owned(g, me), :] = value

        @pl.loop(1, PLANE)
        def _(d):
            gather(g, (me + d) % PLANE, me).start()

    for g in groups:
        @pl.loop(1, PLANE)
        def _(d):
            gather(g, (me + d) % PLANE, (me + PLANE - d) % PLANE).wait_recv()

        back(g, core).start()

    for r in range(1, RAW):
        send_raw(r)

    for g in groups:
        back(g, 1 - core).wait_recv()
        for half in range(CORES):
            for m in range(*GROUPS[g]):
                i, j = PAIRS[half * HALF + m]
                value = total[half, m * TILE:(m + 1) * TILE, :]
                g_ref[i * TILE:(i + 1) * TILE, j * TILE:(j + 1) * TILE] = value
                if i != j:
                    g_ref[j * TILE:(j + 1) * TILE, i * TILE:(i + 1) * TILE] = value.T

    def times(a, b, dims):
        return lax.dot_general(a, b, dims, precision=HIGHEST, preferred_element_type=jnp.float32)

    def inverse_triangle(block_):
        for n, row in enumerate(inverse_factor(times(block_, block_, NT), RANK)):
            s_ref[n:n + 1, :RANK] = row
        return s_ref[:RANK, :RANK]

    @pl.loop(0, SWEEPS - 2)
    def _(sweep):
        block_ref[...] = times(basis_ref[...], g_ref[...], NN)
        basis_ref[...] = times(inverse_triangle(block_ref[...]), block_ref[...], NN)

    block_ref[...] = times(basis_ref[...], g_ref[...], NN)
    last_ref[...] = times(block_ref[...], g_ref[...], NN)
    high, middle, low = three(last_ref[...].T)
    wide_ref[...] = jnp.concatenate([high, middle], axis=1)
    deep_ref[...] = jnp.concatenate([low, high], axis=0)

    def by_last(value):
        high, middle, low = three(value)
        both = lax.dot_general(high, wide_ref[...], NN, preferred_element_type=jnp.float32) + lax.dot_general(
            middle, wide_ref[...], NN, preferred_element_type=jnp.float32)
        return both[:, :RANK] + (both[:, RANK:] + lax.dot_general(
            jnp.concatenate([high, low], axis=1), deep_ref[...], NN, preferred_element_type=jnp.float32))

    def place(c, source):
        return y_ref.at[c // halves, pl.ds((source * halves + c % halves) * pairs, pairs)]

    def send(c, p, source):
        return pltpu.make_async_remote_copy(
            outbox.at[p, pl.ds(c * pairs, pairs)], place(c, source), out_send.at[c, p], out_recv.at[c, source],
            device_id=(wide, p), device_id_type=MESH)

    @pl.loop(RAW, steps)
    def _(c):
        product_ref[...] = by_last(xbuf[pl.ds(pl.multiple_of(c * CHUNK, CHUNK), CHUNK), :])
        for p in range(YS):
            for i in range(2):
                outbox[p, pl.ds(c * pairs + i, count, stride=2), :] = product_ref[pl.ds(2 * p + i, count, stride=width), :]
        for d in (2, 1, 3):
            send(c, (y + d) % YS, y).start()
        y_ref[c // halves, pl.ds(pl.multiple_of((y * halves + c % halves) * pairs, pairs), pairs), :] = outbox[
            y, pl.ds(pl.multiple_of(c * pairs, pairs), pairs), :]

    for r in range(RAW):
        rawin[r, y] = rawbox[r, y]
        for d in (2, 1, 3):
            raw(r, (y + d) % YS, (y + YS - d) % YS).wait_recv()
        value = by_last(jnp.concatenate(
            [jnp.concatenate([rawin[r, source, k] for k in range(N1 // TILE)], axis=1) for source in range(YS)], axis=0))
        for source in range(YS):
            first = (source * halves + r % halves) * pairs
            y_ref[r // halves, first:first + pairs, :] = value[source * pairs:(source + 1) * pairs, :]

    factor_ref[...] = jnp.zeros_like(factor_ref)

    @pl.loop(0, 2)
    def _(sweep):
        inverse = inverse_triangle(block_ref[...])

        @pl.when(sweep == 0)
        def _():
            factor_ref[...] = inverse
            block_ref[...] = times(inverse, last_ref[...], NN)

        @pl.when(sweep == 1)
        def _():
            factor_ref[...] = times(inverse, factor_ref[...], NN)

    for g in groups:
        swap(g).wait_send()
        back(g, core).wait_send()

        @pl.loop(1, PLANE)
        def _(d):
            p = (me + d) % PLANE
            scatter(g, p, me).wait_send()
            gather(g, p, me).wait_send()

        for n in range(len(Z_STEPS)):
            along_z(g, n).wait_send()

    high, middle, low = three(factor_ref[...])
    stacked = jnp.concatenate([jnp.concatenate([high, middle], axis=0)] * 2, axis=1)
    rest = jnp.concatenate([low, high], axis=1)

    def part(c, source):
        return pl.ds(pl.multiple_of((source * halves + c % halves) * pairs, pairs), pairs)

    def store(c, source):
        return pltpu.make_async_copy(
            out_ref.at[c // halves, part(c, source)], out_hbm.at[c // halves, part(c, source)], store_sem.at[c, source])

    def finish(c):
        value = jnp.concatenate([y_ref[c // halves, part(c, source), :] for source in range(YS)], axis=0)
        high_, middle_, low_ = three(value)
        first = lax.dot_general(jnp.concatenate([high_, middle_], axis=1), stacked, NT, preferred_element_type=jnp.float32)
        second = lax.dot_general(jnp.concatenate([high_, low_], axis=1), rest, NT, preferred_element_type=jnp.float32)
        value = first[:, :RANK] + (first[:, RANK:] + second)
        for source in range(YS):
            out_ref[c // halves, part(c, source), :] = value[source * pairs:(source + 1) * pairs, :]
            store(c, source).start()

    @pl.loop(0, RAW)
    def _(r):
        finish(r)

    @pl.loop(RAW, steps)
    def _(c):
        for d in (2, 1, 3):
            send(c, (y + d) % YS, (y + YS - d) % YS).wait_recv()
        finish(c)

    for r in range(RAW):
        for d in (2, 1, 3):
            raw(r, (y + d) % YS, y).wait_send()

    @pl.loop(RAW, steps)
    def _(c):
        for d in (2, 1, 3):
            send(c, (y + d) % YS, y).wait_send()

    @pl.loop(0, steps)
    def _(c):
        for source in range(YS):
            store(c, source).wait()


def copy_kernel(y_hbm, out_hbm, y_ref, sem):
    steps = y_ref.shape[0]

    def load(c):
        return pltpu.make_async_copy(y_hbm.at[c], y_ref.at[c], sem.at[0, c])

    def store(c):
        return pltpu.make_async_copy(y_ref.at[c], out_hbm.at[c], sem.at[1, c])

    for c in range(steps):
        load(c).start()
    for c in range(steps):
        load(c).wait()
        store(c).start()
    for c in range(steps):
        store(c).wait()


def per_device(fields, start_basis):
    nv, n2, n3, n1 = fields.shape
    unfolded = fields.reshape(-1, n1)
    rows = unfolded.shape[0]
    steps = rows // CHUNK
    stages = len(GROUPS)
    y = pl.pallas_call(
        functools.partial(tucker_kernel, nv),
        out_shape=jax.ShapeDtypeStruct((nv, rows // nv, RANK), jnp.float32),
        in_specs=[pl.BlockSpec(memory_space=pltpu.HBM)] * 2,
        out_specs=pl.BlockSpec(memory_space=pltpu.HBM),
        scratch_shapes=[
            pltpu.VMEM((rows, n1), jnp.float32),
            pltpu.VMEM((nv, rows // nv, RANK), jnp.float32),
            pltpu.VMEM((nv, rows // nv, RANK), jnp.float32),
            pltpu.VMEM((n1, RANK), jnp.float32),
            pltpu.VMEM((RANK, RANK), jnp.float32),
            pltpu.VMEM((RAW, YS, n1 // TILE, CHUNK // YS, TILE), jnp.float32),
            pltpu.VMEM((RAW, YS, n1 // TILE, CHUNK // YS, TILE), jnp.float32),
            pltpu.VMEM((n1, n1), jnp.float32),
            pltpu.VMEM((RANK, n1), jnp.float32),
            pltpu.VMEM((RANK, n1), jnp.float32),
            pltpu.VMEM((RANK, n1), jnp.float32),
            pltpu.VMEM((n1, 2 * RANK), jnp.bfloat16),
            pltpu.VMEM((2 * n1, RANK), jnp.bfloat16),
            pltpu.VMEM((CHUNK, RANK), jnp.float32),
            pltpu.VMEM((YS, rows // YS, RANK), jnp.float32),
            pltpu.VMEM((n1, n1), jnp.float32),
            pltpu.VMEM((HALF * TILE, TILE), jnp.float32),
            pltpu.VMEM((HALF * TILE, TILE), jnp.float32),
            pltpu.VMEM((HALF * TILE, TILE), jnp.float32),
            pltpu.VMEM((CORES, HALF * TILE, TILE), jnp.float32),
            pltpu.VMEM((PLANE, HALF * OWN, TILE), jnp.float32),
            pltpu.VMEM((7, HALF * OWN, TILE), jnp.float32),
            pltpu.SemaphoreType.DMA((steps,)),
            pltpu.SemaphoreType.DMA((2, stages)),
            pltpu.SemaphoreType.DMA((stages, PLANE)),
            pltpu.SemaphoreType.DMA((stages, PLANE)),
            pltpu.SemaphoreType.DMA((stages, len(Z_STEPS))),
            pltpu.SemaphoreType.DMA((stages, len(Z_STEPS))),
            pltpu.SemaphoreType.DMA((stages, PLANE)),
            pltpu.SemaphoreType.DMA((stages, PLANE)),
            pltpu.SemaphoreType.DMA((2, stages)),
            pltpu.SemaphoreType.DMA((steps, YS)),
            pltpu.SemaphoreType.DMA((steps, YS)),
            pltpu.SemaphoreType.DMA((steps, YS)),
            pltpu.SemaphoreType.DMA((1,)),
            pltpu.SemaphoreType.DMA((RAW, YS)),
            pltpu.SemaphoreType.DMA((RAW, YS)),
        ],
        compiler_params=pltpu.CompilerParams(collective_id=0, has_side_effects=True, vmem_limit_bytes=67043328),
    )(unfolded, start_basis)
    parts = (2, rows // 2, RANK)
    out = pl.pallas_call(
        copy_kernel,
        out_shape=jax.ShapeDtypeStruct(parts, jnp.float32),
        in_specs=[pl.BlockSpec(memory_space=pltpu.HBM)],
        out_specs=pl.BlockSpec(memory_space=pltpu.HBM),
        scratch_shapes=[pltpu.VMEM(parts, jnp.float32), pltpu.SemaphoreType.DMA((2, 2))],
    )(y.reshape(parts))
    return out.reshape(nv, n2 * YS, n3 // YS, RANK)


def solution(mesh):
    in_specs = (P(None, "slab", "wide", None), P())
    out_specs = P(None, None, ("wide", "slab"), None)
    return jax.shard_map(
        per_device, mesh=mesh, in_specs=in_specs, out_specs=out_specs, check_vma=False
    )
```

```python
import functools

import jax
import jax.numpy as jnp
from jax import lax
from jax.experimental import pallas as pl
from jax.experimental.pallas import tpu as pltpu
from jax.sharding import PartitionSpec as P

SWEEPS = 4
MESH = pl.DeviceIdType.MESH
CORES, XS, ZS, YS = 2, 4, 8, 4
PLANE = XS * YS
N1 = 512
TILE = 128
PAIRS = [(i, j) for i in range(N1 // TILE) for j in range(i, N1 // TILE)]
HALF = len(PAIRS) // CORES
OWN = TILE // PLANE
GROUPS = ((0, 3), (3, HALF))
CHUNK = 512
SUB = 8
RAW = 2
PIECES = RAW * (N1 // TILE)
EARLY = 2
MIDDLE = 5
Z_STEPS = (1, -1, -3, 3)
Z_SOURCE = (0, 0, 3, 4)
Z_TARGET = (1, 2, 5, 6)
RANK = 128
HIGHEST = lax.Precision.HIGHEST
NT = (((1,), (1,)), ((), ()))
TN = (((0,), (0,)), ((), ()))
NN = (((1,), (0,)), ((), ()))


def inverse_factor(square, n):
    blocks = n // SUB
    lane = lax.broadcasted_iota(jnp.int32, (SUB, n), 1)
    sub = lax.broadcasted_iota(jnp.int32, (SUB, n), 0)
    a = [square[SUB * i:SUB * (i + 1), :] for i in range(blocks)]
    j = [(lane == sub + SUB * i).astype(jnp.float32) for i in range(blocks)]
    rows = []

    def along_lanes(v, c):
        return jnp.broadcast_to(v[:, c:c + 1], (SUB, n))

    def along_sublanes(v, p):
        return jnp.broadcast_to(v[p:p + 1, :], (SUB, n))

    for k in range(blocks):
        cols = [along_lanes(a[k], SUB * k + p) for p in range(SUB)]
        e = {(i, p): along_sublanes(cols[p], i) for p in range(SUB) for i in range(p, SUB)}
        r, l = [], {}
        for p in range(SUB):
            r.append(lax.rsqrt(e[p, p]))
            for i in range(p + 1, SUB):
                l[i, p] = e[i, p] * r[p]
            for q in range(p + 1, SUB):
                for i in range(q, SUB):
                    e[i, q] = e[i, q] - l[i, p] * l[q, p]

        def forward(values):
            out = []
            for p in range(SUB):
                v = values[p]
                for q in range(p):
                    v = v - l[p, q] * out[q]
                out.append(v * r[p])
            return out

        upper = forward([along_sublanes(a[k], p) for p in range(SUB)])
        inverse = forward([along_sublanes(j[k], p) for p in range(SUB)])
        rows.extend(v[:1] for v in inverse)
        for i in range(k + 1, blocks):
            lower = forward([along_lanes(a[i], SUB * k + p) for p in range(SUB)])
            for p in range(SUB):
                a[i] = a[i] - lower[p] * upper[p]
                j[i] = j[i] - lower[p] * inverse[p]
    return rows


def three(value):
    high = value.astype(jnp.bfloat16)
    rest = value - high.astype(jnp.float32)
    middle = rest.astype(jnp.bfloat16)
    return high, middle, (rest - middle.astype(jnp.float32)).astype(jnp.bfloat16)


def tucker_kernel(nv, x_hbm, start_hbm, out_hbm, xbuf, y_ref, out_ref, start_ref, factor_ref, rawbox, rawin, g_ref, basis_ref, block_ref, last_ref, wide_ref, deep_ref, product_ref, outbox, s_ref, mine,
                  theirs, inbox, total, parts, zparts, load_sem, swap_sem, rs_send, rs_recv, z_send, z_recv, ag_send, ag_recv,
                  back_sem, out_send, out_recv, store_sem, side_sem, raw_send, raw_recv):
    wide = lax.axis_index("wide")
    y = lax.axis_index("slab")
    core = wide % CORES
    x = (wide // CORES) % XS
    z = wide // (CORES * XS)
    me = x * YS + y
    sibling = (wide + 1 - 2 * core, y)
    groups = range(len(GROUPS))

    def plane_device(p):
        return ((z * XS + p // YS) * CORES + core, p % YS)

    def z_device(q):
        return ((q * XS + x) * CORES + core, y)

    barrier = pltpu.get_barrier_semaphore()
    pl.semaphore_signal(barrier, inc=1, device_id=sibling, device_id_type=MESH)

    @pl.loop(1, PLANE)
    def _(d):
        pl.semaphore_signal(barrier, inc=1, device_id=plane_device((me + d) % PLANE), device_id_type=MESH)

    for step in Z_STEPS:
        pl.semaphore_signal(barrier, inc=1, device_id=z_device((z + ZS + step) % ZS), device_id_type=MESH)

    rows = x_hbm.shape[0]
    steps = rows // CHUNK

    def load(c):
        return pltpu.make_async_copy(x_hbm.at[pl.ds(c * CHUNK, CHUNK)], xbuf.at[pl.ds(c * CHUNK, CHUNK)], load_sem.at[c])

    for c in range(steps):
        load(c).start()
    load_start = pltpu.make_async_copy(start_hbm, start_ref, side_sem.at[0])
    load_start.start()
    s_ref[...] = jnp.zeros_like(s_ref)

    def add_slice(c):
        value = xbuf[pl.ds(pl.multiple_of(c * CHUNK, CHUNK), CHUNK), :]
        high = value.astype(jnp.bfloat16)
        low = (value - high.astype(jnp.float32)).astype(jnp.bfloat16)
        s_ref[...] += 0.5 * lax.dot_general(high, high, TN, preferred_element_type=jnp.float32) + lax.dot_general(
            high, low, TN, preferred_element_type=jnp.float32)

    load_start.wait()
    basis_ref[...] = start_ref[...].T
    width = 2 * YS
    count = CHUNK // width
    pairs = CHUNK // YS
    halves = steps // nv

    columns = N1 // TILE

    def sort_raw(n):
        r, k = n // columns, n % columns
        product_ref[...] = xbuf[r * CHUNK:(r + 1) * CHUNK, k * TILE:(k + 1) * TILE]
        for p in range(YS):
            for i in range(2):
                rawbox[n, p, pl.ds(i, count, stride=2), :] = product_ref[pl.ds(2 * p + i, count, stride=width), :]

    def raw(n, p, source):
        return pltpu.make_async_remote_copy(
            rawbox.at[n, p], rawin.at[n, source], raw_send.at[n, p], raw_recv.at[n, source], device_id=(wide, p), device_id_type=MESH)

    def send_raw(first, last):
        @pl.loop(first, last)
        def _(n):
            for d in (2, 1, 3):
                raw(n, (y + d) % YS, y).start()

    load(0).wait()
    for n in range(EARLY):
        sort_raw(n)
    pl.semaphore_wait(barrier, PLANE + len(Z_STEPS))
    send_raw(0, EARLY)
    add_slice(0)

    @pl.loop(1, steps)
    def _(c):
        load(c).wait()
        add_slice(c)

    scale = 1.0 / (rows * PLANE * ZS * CORES)

    def block(n):
        i, j = PAIRS[n]
        a = s_ref[i * TILE:(i + 1) * TILE, j * TILE:(j + 1) * TILE]
        b = s_ref[j * TILE:(j + 1) * TILE, i * TILE:(i + 1) * TILE]
        return (a + b.T) * scale

    def span(g):
        first, last = GROUPS[g]
        return pl.ds(first * TILE, (last - first) * TILE)

    def share(g):
        first, last = GROUPS[g]
        return pl.ds(first * OWN, (last - first) * OWN)

    def owned(g, p):
        first, last = GROUPS[g]
        return pl.ds(pl.multiple_of(first * TILE + p * ((last - first) * OWN), SUB), (last - first) * OWN)

    def swap(g):
        return pltpu.make_async_remote_copy(
            theirs.at[span(g)], inbox.at[span(g)], swap_sem.at[0, g], swap_sem.at[1, g], device_id=sibling, device_id_type=MESH)

    for g in groups:
        for c in range(CORES):
            @pl.when(core == c)
            def _():
                for n in range(*GROUPS[g]):
                    theirs[n * TILE:(n + 1) * TILE, :] = block((1 - c) * HALF + n)
        swap(g).start()
    for c in range(CORES):
        @pl.when(core == c)
        def _():
            for n in range(HALF):
                mine[n * TILE:(n + 1) * TILE, :] = block(c * HALF + n)
    for n in range(EARLY, PIECES):
        sort_raw(n)

    def scatter(g, p, source):
        return pltpu.make_async_remote_copy(
            mine.at[owned(g, p)], parts.at[source, share(g)], rs_send.at[g, p], rs_recv.at[g, source],
            device_id=plane_device(p), device_id_type=MESH)

    def along_z(g, n):
        return pltpu.make_async_remote_copy(
            zparts.at[Z_SOURCE[n], share(g)], zparts.at[Z_TARGET[n], share(g)], z_send.at[g, n], z_recv.at[g, n],
            device_id=z_device((z + ZS + Z_STEPS[n]) % ZS), device_id_type=MESH)

    done = total.at[core]

    def gather(g, p, source):
        return pltpu.make_async_remote_copy(
            done.at[owned(g, source)], done.at[owned(g, source)], ag_send.at[g, p], ag_recv.at[g, source],
            device_id=plane_device(p), device_id_type=MESH)

    def back(g, c):
        return pltpu.make_async_remote_copy(
            total.at[c, span(g)], total.at[c, span(g)], back_sem.at[0, g], back_sem.at[1, g], device_id=sibling, device_id_type=MESH)

    for g in groups:
        swap(g).wait_recv()
        mine[span(g), :] += inbox[span(g), :]

        @pl.loop(1, PLANE)
        def _(d):
            scatter(g, (me + d) % PLANE, me).start()

    for g in groups:
        zparts[0, share(g), :] = mine[owned(g, me), :]

        @pl.loop(1, PLANE)
        def _(d):
            source = (me + PLANE - d) % PLANE
            scatter(g, (me + d) % PLANE, source).wait_recv()
            zparts[0, share(g), :] += parts[source, share(g), :]

        for n in (0, 1):
            along_z(g, n).start()

    send_raw(EARLY, MIDDLE)

    for g in groups:
        for n in (0, 1):
            along_z(g, n).wait_recv()
        two = zparts[0, share(g), :] + zparts[2, share(g), :]
        zparts[4, share(g), :] = two
        zparts[3, share(g), :] = two + zparts[1, share(g), :]
        for n in (2, 3):
            along_z(g, n).start()

    for g in groups:
        for n in (2, 3):
            along_z(g, n).wait_recv()
        value = zparts[3, share(g), :] + (zparts[5, share(g), :] + zparts[6, share(g), :])
        done[owned(g, me), :] = value

        @pl.loop(1, PLANE)
        def _(d):
            gather(g, (me + d) % PLANE, me).start()

    for g in groups:
        @pl.loop(1, PLANE)
        def _(d):
            gather(g, (me + d) % PLANE, (me + PLANE - d) % PLANE).wait_recv()

        back(g, core).start()

    send_raw(MIDDLE, PIECES)

    for g in groups:
        back(g, 1 - core).wait_recv()
        for half in range(CORES):
            for m in range(*GROUPS[g]):
                i, j = PAIRS[half * HALF + m]
                value = total[half, m * TILE:(m + 1) * TILE, :]
                g_ref[i * TILE:(i + 1) * TILE, j * TILE:(j + 1) * TILE] = value
                if i != j:
                    g_ref[j * TILE:(j + 1) * TILE, i * TILE:(i + 1) * TILE] = value.T

    def times(a, b, dims):
        return lax.dot_general(a, b, dims, precision=HIGHEST, preferred_element_type=jnp.float32)

    def inverse_triangle(block_):
        for n, row in enumerate(inverse_factor(times(block_, block_, NT), RANK)):
            s_ref[n:n + 1, :RANK] = row
        return s_ref[:RANK, :RANK]

    @pl.loop(0, SWEEPS - 2)
    def _(sweep):
        block_ref[...] = times(basis_ref[...], g_ref[...], NN)
        basis_ref[...] = times(inverse_triangle(block_ref[...]), block_ref[...], NN)

    block_ref[...] = times(basis_ref[...], g_ref[...], NN)
    last_ref[...] = times(block_ref[...], g_ref[...], NN)
    high, middle, low = three(last_ref[...].T)
    wide_ref[...] = jnp.concatenate([high, middle], axis=1)
    deep_ref[...] = jnp.concatenate([low, high], axis=0)

    def by_last(value):
        high, middle, low = three(value)
        both = lax.dot_general(high, wide_ref[...], NN, preferred_element_type=jnp.float32) + lax.dot_general(
            middle, wide_ref[...], NN, preferred_element_type=jnp.float32)
        return both[:, :RANK] + (both[:, RANK:] + lax.dot_general(
            jnp.concatenate([high, low], axis=1), deep_ref[...], NN, preferred_element_type=jnp.float32))

    def place(c, source):
        return y_ref.at[c // halves, pl.ds((source * halves + c % halves) * pairs, pairs)]

    def send(c, p, source):
        return pltpu.make_async_remote_copy(
            outbox.at[p, pl.ds(c * pairs, pairs)], place(c, source), out_send.at[c, p], out_recv.at[c, source],
            device_id=(wide, p), device_id_type=MESH)

    @pl.loop(RAW, steps)
    def _(c):
        product_ref[...] = by_last(xbuf[pl.ds(pl.multiple_of(c * CHUNK, CHUNK), CHUNK), :])
        for p in range(YS):
            for i in range(2):
                outbox[p, pl.ds(c * pairs + i, count, stride=2), :] = product_ref[pl.ds(2 * p + i, count, stride=width), :]
        for d in (2, 1, 3):
            send(c, (y + d) % YS, y).start()
        y_ref[c // halves, pl.ds(pl.multiple_of((y * halves + c % halves) * pairs, pairs), pairs), :] = outbox[
            y, pl.ds(pl.multiple_of(c * pairs, pairs), pairs), :]

    @pl.loop(0, PIECES)
    def _(n):
        rawin[n, y] = rawbox[n, y]
        for d in (2, 1, 3):
            raw(n, (y + d) % YS, (y + YS - d) % YS).wait_recv()

    for r in range(RAW):
        value = by_last(jnp.concatenate(
            [jnp.concatenate([rawin[r * columns + k, source] for k in range(columns)], axis=1) for source in range(YS)], axis=0))
        for source in range(YS):
            first = (source * halves + r % halves) * pairs
            y_ref[r // halves, first:first + pairs, :] = value[source * pairs:(source + 1) * pairs, :]

    factor_ref[...] = jnp.zeros_like(factor_ref)

    @pl.loop(0, 2)
    def _(sweep):
        inverse = inverse_triangle(block_ref[...])

        @pl.when(sweep == 0)
        def _():
            factor_ref[...] = inverse
            block_ref[...] = times(inverse, last_ref[...], NN)

        @pl.when(sweep == 1)
        def _():
            factor_ref[...] = times(inverse, factor_ref[...], NN)

    for g in groups:
        swap(g).wait_send()
        back(g, core).wait_send()

        @pl.loop(1, PLANE)
        def _(d):
            p = (me + d) % PLANE
            scatter(g, p, me).wait_send()
            gather(g, p, me).wait_send()

        for n in range(len(Z_STEPS)):
            along_z(g, n).wait_send()

    high, middle, low = three(factor_ref[...])
    stacked = jnp.concatenate([jnp.concatenate([high, middle], axis=0)] * 2, axis=1)
    rest = jnp.concatenate([low, high], axis=1)

    def part(c, source):
        return pl.ds(pl.multiple_of((source * halves + c % halves) * pairs, pairs), pairs)

    def store(c, source):
        return pltpu.make_async_copy(
            out_ref.at[c // halves, part(c, source)], out_hbm.at[c // halves, part(c, source)], store_sem.at[c, source])

    def finish(c):
        value = jnp.concatenate([y_ref[c // halves, part(c, source), :] for source in range(YS)], axis=0)
        high_, middle_, low_ = three(value)
        first = lax.dot_general(jnp.concatenate([high_, middle_], axis=1), stacked, NT, preferred_element_type=jnp.float32)
        second = lax.dot_general(jnp.concatenate([high_, low_], axis=1), rest, NT, preferred_element_type=jnp.float32)
        value = first[:, :RANK] + (first[:, RANK:] + second)
        for source in range(YS):
            out_ref[c // halves, part(c, source), :] = value[source * pairs:(source + 1) * pairs, :]
            store(c, source).start()

    @pl.loop(0, RAW)
    def _(r):
        finish(r)

    @pl.loop(RAW, steps)
    def _(c):
        for d in (2, 1, 3):
            send(c, (y + d) % YS, (y + YS - d) % YS).wait_recv()
        finish(c)

    @pl.loop(0, PIECES)
    def _(n):
        for d in (2, 1, 3):
            raw(n, (y + d) % YS, y).wait_send()

    @pl.loop(RAW, steps)
    def _(c):
        for d in (2, 1, 3):
            send(c, (y + d) % YS, y).wait_send()

    @pl.loop(0, steps)
    def _(c):
        for source in range(YS):
            store(c, source).wait()


def copy_kernel(y_hbm, out_hbm, y_ref, sem):
    steps = y_ref.shape[0]

    def load(c):
        return pltpu.make_async_copy(y_hbm.at[c], y_ref.at[c], sem.at[0, c])

    def store(c):
        return pltpu.make_async_copy(y_ref.at[c], out_hbm.at[c], sem.at[1, c])

    for c in range(steps):
        load(c).start()
    for c in range(steps):
        load(c).wait()
        store(c).start()
    for c in range(steps):
        store(c).wait()


def per_device(fields, start_basis):
    nv, n2, n3, n1 = fields.shape
    unfolded = fields.reshape(-1, n1)
    rows = unfolded.shape[0]
    steps = rows // CHUNK
    stages = len(GROUPS)
    y = pl.pallas_call(
        functools.partial(tucker_kernel, nv),
        out_shape=jax.ShapeDtypeStruct((nv, rows // nv, RANK), jnp.float32),
        in_specs=[pl.BlockSpec(memory_space=pltpu.HBM)] * 2,
        out_specs=pl.BlockSpec(memory_space=pltpu.HBM),
        scratch_shapes=[
            pltpu.VMEM((rows, n1), jnp.float32),
            pltpu.VMEM((nv, rows // nv, RANK), jnp.float32),
            pltpu.VMEM((nv, rows // nv, RANK), jnp.float32),
            pltpu.VMEM((n1, RANK), jnp.float32),
            pltpu.VMEM((RANK, RANK), jnp.float32),
            pltpu.VMEM((PIECES, YS, CHUNK // YS, TILE), jnp.float32),
            pltpu.VMEM((PIECES, YS, CHUNK // YS, TILE), jnp.float32),
            pltpu.VMEM((n1, n1), jnp.float32),
            pltpu.VMEM((RANK, n1), jnp.float32),
            pltpu.VMEM((RANK, n1), jnp.float32),
            pltpu.VMEM((RANK, n1), jnp.float32),
            pltpu.VMEM((n1, 2 * RANK), jnp.bfloat16),
            pltpu.VMEM((2 * n1, RANK), jnp.bfloat16),
            pltpu.VMEM((CHUNK, RANK), jnp.float32),
            pltpu.VMEM((YS, rows // YS, RANK), jnp.float32),
            pltpu.VMEM((n1, n1), jnp.float32),
            pltpu.VMEM((HALF * TILE, TILE), jnp.float32),
            pltpu.VMEM((HALF * TILE, TILE), jnp.float32),
            pltpu.VMEM((HALF * TILE, TILE), jnp.float32),
            pltpu.VMEM((CORES, HALF * TILE, TILE), jnp.float32),
            pltpu.VMEM((PLANE, HALF * OWN, TILE), jnp.float32),
            pltpu.VMEM((7, HALF * OWN, TILE), jnp.float32),
            pltpu.SemaphoreType.DMA((steps,)),
            pltpu.SemaphoreType.DMA((2, stages)),
            pltpu.SemaphoreType.DMA((stages, PLANE)),
            pltpu.SemaphoreType.DMA((stages, PLANE)),
            pltpu.SemaphoreType.DMA((stages, len(Z_STEPS))),
            pltpu.SemaphoreType.DMA((stages, len(Z_STEPS))),
            pltpu.SemaphoreType.DMA((stages, PLANE)),
            pltpu.SemaphoreType.DMA((stages, PLANE)),
            pltpu.SemaphoreType.DMA((2, stages)),
            pltpu.SemaphoreType.DMA((steps, YS)),
            pltpu.SemaphoreType.DMA((steps, YS)),
            pltpu.SemaphoreType.DMA((steps, YS)),
            pltpu.SemaphoreType.DMA((1,)),
            pltpu.SemaphoreType.DMA((PIECES, YS)),
            pltpu.SemaphoreType.DMA((PIECES, YS)),
        ],
        compiler_params=pltpu.CompilerParams(collective_id=0, has_side_effects=True, vmem_limit_bytes=67043328),
    )(unfolded, start_basis)
    parts = (2, rows // 2, RANK)
    out = pl.pallas_call(
        copy_kernel,
        out_shape=jax.ShapeDtypeStruct(parts, jnp.float32),
        in_specs=[pl.BlockSpec(memory_space=pltpu.HBM)],
        out_specs=pl.BlockSpec(memory_space=pltpu.HBM),
        scratch_shapes=[pltpu.VMEM(parts, jnp.float32), pltpu.SemaphoreType.DMA((2, 2))],
    )(y.reshape(parts))
    return out.reshape(nv, n2 * YS, n3 // YS, RANK)


def solution(mesh):
    in_specs = (P(None, "slab", "wide", None), P())
    out_specs = P(None, None, ("wide", "slab"), None)
    return jax.shard_map(
        per_device, mesh=mesh, in_specs=in_specs, out_specs=out_specs, check_vma=False
    )
```
